32 devices in a mesh: fsdp: 2 (over x), rep: 16 (over z, y, core).
Axes of the slice: x: 2, y: 2, z: 4, core: 2. Of those that a mesh axis runs over, the one named last changes fastest.
Arguments:
- images: bfloat16 [128, 197, 384], P(('fsdp', 'rep')), may hold values from -5 to 5
- cotangent: bfloat16 [128, 197, 384], P(('fsdp', 'rep')), may hold values from -6 to 6
- weights: float32 [1777664], P('fsdp'), may hold values from -3 to 3
- first_moment: float32 [1777664], P(('fsdp', 'rep'))
- second_moment: float32 [1777664], P(('fsdp', 'rep')), as said below
Outputs:
- output: bfloat16 [128, 197, 384], P(('fsdp', 'rep'))
- input_grad: bfloat16 [128, 197, 384], P(('fsdp', 'rep'))
- new_weights: float32 [1777664], P('fsdp')
- gradients: float32 [1777664], P(('fsdp', 'rep'))
- new_first: float32 [1777664], P(('fsdp', 'rep'))
- new_second: float32 [1777664], P(('fsdp', 'rep'))
The draws below stay inside these ranges and needn't reach their ends.
Inputs may be any that keep to these rules, and one draw needn't show every extreme that they name: second_moment is positive.
All inputs are finite; a program needn't handle non-finite values.
Results may differ from the reference program's by a relative error of at most 0.0095.
The reference program's roundings to bfloat16 on the way count: a program that leaves them out, or rounds other values in their place, can miss the bound.
Values may be sent and summed in bfloat16 or wider, within the bound.
A program may use at most 128 MiB of HBM per device.

```python
import math
import jax
import jax.numpy as jnp
from jax import lax

D = 384
H = 6
FF = 1536
SEQ = 197
IMAGES = 128
TOKENS = 25216
PARAMS = 1774080
FLAT = 1777664


def rough(key, shape):
    return jnp.clip(jax.random.normal(key, shape, jnp.float32), -5.0, 5.0)


def draw_images(key, part):
    keys = jax.random.split(key, 1)
    base = rough(keys[0], (IMAGES, SEQ, D))
    return base.astype(jnp.bfloat16)


def draw_weights(key, part):
    keys = jax.random.split(key, 10)
    inv_width = D ** (-0.5)
    query_w = rough(keys[0], (D, D)) * inv_width
    key_w = rough(keys[1], (D, D)) * inv_width
    value_w = rough(keys[2], (D, D)) * inv_width
    proj_w = rough(keys[3], (D, D)) * (8.0 * inv_width)
    fc1_w = rough(keys[4], (D, FF)) * inv_width
    fc2_w = rough(keys[5], (FF, D)) * FF ** (-0.5)
    gains = jax.random.uniform(keys[6], (2, D), jnp.float32, 0.6, 1.4)
    shifts = rough(keys[7], (6, D)) * 0.3
    vectors = jnp.stack([gains[0], shifts[0], shifts[1], shifts[2], shifts[3], gains[1], shifts[4], shifts[5]])
    bias_one = rough(keys[8], (FF,)) * 0.3
    tail = rough(keys[9], (FLAT - PARAMS,)) * 0.05
    qkv_w = jnp.concatenate([query_w, key_w, value_w], 1)
    whole = jnp.concatenate([qkv_w.reshape(-1), proj_w.reshape(-1), fc1_w.reshape(-1), fc2_w.reshape(-1), vectors.reshape(-1), bias_one, tail])
    return jnp.clip(whole, -3.0, 3.0)


def moment_scale():
    layout = [(3 * D * D, 1.0), (D * D, 0.15), (D * FF, 0.3), (FF * D, 0.6), (2 * D, 1.7), (3 * D, 1.0), (2 * D, 0.6), (D, 1.0), (FF, 0.3), (FLAT - PARAMS, 1.0)]
    parts_list = [jnp.full((count,), level, jnp.float32) for count, level in layout]
    return jnp.concatenate(parts_list) * TOKENS ** 0.5


def draw_first_moment(key, part):
    return 0.05 * moment_scale() * rough(key, (FLAT,))


def draw_second_moment(key, part):
    spread = jnp.exp(jax.random.uniform(key, (FLAT,), jnp.float32, -1.4, 1.4))
    level = moment_scale()
    return 0.0005 * level * level * spread


def level_of(stream_key, dims, cuts, smallest, high):
    def one(dim, parts):
        steps = jax.random.uniform(jax.random.fold_in(jax.random.fold_in(stream_key, 6), dim), (parts,), jnp.float32, smallest / len(cuts), high / len(cuts))
        return jnp.repeat(jnp.exp(steps), dims[dim] // parts).reshape((-1,) + (1,) * (len(dims) - dim - 1))

    factor_of = one(*cuts[0])
    for cut in cuts[1:]:
        factor_of = factor_of * one(*cut)
    return factor_of


def bell_draw(own_key, shape, scale, limit, cuts=(), held_as=jnp.bfloat16):
    level = level_of(own_key, shape, cuts, -0.22, 0.18) if cuts else 1.0
    values = jax.random.normal(own_key, shape, jnp.float32) * scale * level
    return jnp.minimum(jnp.maximum(values, -limit), limit).astype(held_as)


def setup_inputs(seed: int = 0) -> dict:
    seeds = jax.random.split(jax.random.key(seed), 6)
    return {
        "images": draw_images(jax.random.fold_in(seeds[5], 71), 0),
        "cotangent": bell_draw(seeds[1], (IMAGES, SEQ, D), 1.0, 6.0, ((0, 32),)),
        "weights": draw_weights(jax.random.fold_in(seeds[5], 71), 0),
        "first_moment": draw_first_moment(jax.random.fold_in(seeds[5], 71), 0),
        "second_moment": draw_second_moment(jax.random.fold_in(seeds[5], 71), 0),
    }


norm_eps = 1e-06
half_root = 0.7071067811865476
inv_root_two_pi = 0.3989422804014327
beta_one = 0.9
beta_two = 0.999
learn_rate = 0.02
decay_rate = 0.05
adam_eps = 1e-08

def product(form, left, right):
    return jnp.einsum(form, left.astype(jnp.float32), right.astype(jnp.float32))

def layer_norm_forward(values):
    centred = values - lax.optimization_barrier(jnp.mean(values, -1, keepdims=True))
    variance = lax.optimization_barrier(jnp.mean(centred * centred, -1, keepdims=True))
    inverse = lax.rsqrt(variance + norm_eps)
    return (centred * inverse, inverse)

def layer_norm_backward(d_scaled, scaled, inverse):
    first_mean = lax.optimization_barrier(jnp.mean(d_scaled, -1, keepdims=True))
    second_mean = lax.optimization_barrier(jnp.mean(d_scaled * scaled, -1, keepdims=True))
    return (d_scaled - first_mean - scaled * second_mean) * inverse

def unpack(flat_vec):
    edge_one = 3 * D * D
    edge_two = edge_one + D * D
    edge_three = edge_two + D * FF
    edge_four = edge_three + FF * D
    edge_five = edge_four + 8 * D
    w_qkv = flat_vec[:edge_one].reshape(D, 3 * D)
    w_proj = flat_vec[edge_one:edge_two].reshape(D, D)
    w_fc1 = flat_vec[edge_two:edge_three].reshape(D, FF)
    w_fc2 = flat_vec[edge_three:edge_four].reshape(FF, D)
    vectors = flat_vec[edge_four:edge_five].reshape(8, D)
    b_fc1 = flat_vec[edge_five:edge_five + FF]
    return (w_qkv, w_proj, w_fc1, w_fc2, vectors, b_fc1)

def pack(grads, length):
    pieces = [grad.reshape(-1) for grad in grads]
    used = sum((piece_arr.shape[0] for piece_arr in pieces))
    pieces.append(jnp.zeros((length - used,), jnp.float32))
    return jnp.concatenate(pieces)

def layer_block(images, cotangent, fwd_params, bwd_params):
    w_qkv, w_proj, w_fc1, w_fc2, vectors, b_fc1 = fwd_params
    back_qkv, back_proj, back_fc1, back_fc2, back_vectors, back_b1 = bwd_params
    batch, length, width = images.shape
    head_size = width // H
    token_rows = batch * length
    scale = head_size ** (-0.5)
    vector_float = vectors.astype(jnp.float32)
    backward_vector_slice = back_vectors.astype(jnp.float32)
    input_token_rows = images.astype(jnp.float32).reshape(token_rows, width)
    first_centered_scaled, first_inverse_deviation = layer_norm_forward(input_token_rows)
    first_normed_rows = (first_centered_scaled * vector_float[0] + vector_float[1]).astype(jnp.bfloat16)
    qkv_rows = jnp.dot(first_normed_rows, w_qkv, preferred_element_type=jnp.float32)
    query = (qkv_rows[:, :width] + vector_float[2]).astype(jnp.bfloat16).reshape(batch, length, H, head_size)
    key_arr = qkv_rows[:, width:2 * width].astype(jnp.bfloat16).reshape(batch, length, H, head_size)
    value = (qkv_rows[:, 2 * width:] + vector_float[3]).astype(jnp.bfloat16).reshape(batch, length, H, head_size)
    scores = product('bqhd,bkhd->bhqk', query, key_arr) * scale
    top_score = lax.optimization_barrier(jnp.max(scores, -1, keepdims=True))
    log_total = top_score + jnp.log(lax.optimization_barrier(jnp.sum(jnp.exp(scores - top_score), -1, keepdims=True)))
    probs_bf = jnp.exp(scores - log_total).astype(jnp.bfloat16)
    mixed = product('bhqk,bkhd->bqhd', probs_bf, value).astype(jnp.bfloat16).reshape(token_rows, width)
    residual_stream = input_token_rows + jnp.dot(mixed, w_proj, preferred_element_type=jnp.float32) + vector_float[4]
    second_centered_scaled, second_inverse_deviation = layer_norm_forward(residual_stream)
    second_normed_rows = (second_centered_scaled * vector_float[5] + vector_float[6]).astype(jnp.bfloat16)
    preact = jnp.dot(second_normed_rows, w_fc1, preferred_element_type=jnp.float32) + b_fc1.astype(jnp.float32)
    normal_cdf = 0.5 * (1.0 + jax.scipy.special.erf(preact * half_root))
    activ = (preact * normal_cdf).astype(jnp.bfloat16)
    result = residual_stream + jnp.dot(activ, w_fc2, preferred_element_type=jnp.float32) + vector_float[7]
    d_out = cotangent.reshape(token_rows, width)
    output_gradient_float = d_out.astype(jnp.float32)
    grad_fc2 = jnp.dot(activ.T, d_out, preferred_element_type=jnp.float32)
    grad_bias2 = lax.optimization_barrier(jnp.sum(output_gradient_float, 0))
    d_act = jnp.dot(d_out, back_fc2.T, preferred_element_type=jnp.float32)
    d_pre = d_act * (normal_cdf + preact * jnp.exp(-0.5 * preact * preact) * inv_root_two_pi)
    grad_bias1 = lax.optimization_barrier(jnp.sum(d_pre, 0))
    d_pre_bf = d_pre.astype(jnp.bfloat16)
    grad_fc1 = jnp.dot(second_normed_rows.T, d_pre_bf, preferred_element_type=jnp.float32)
    second_norm_gradient = jnp.dot(d_pre_bf, back_fc1.T, preferred_element_type=jnp.float32)
    gain2_gradient = lax.optimization_barrier(jnp.sum(second_norm_gradient * second_centered_scaled, 0))
    grad_shift2 = lax.optimization_barrier(jnp.sum(second_norm_gradient, 0))
    residual_gradient = output_gradient_float + layer_norm_backward(second_norm_gradient * backward_vector_slice[5], second_centered_scaled, second_inverse_deviation)
    grad_pbias = lax.optimization_barrier(jnp.sum(residual_gradient, 0))
    d_resid_bf = residual_gradient.astype(jnp.bfloat16)
    grad_proj = jnp.dot(mixed.T, d_resid_bf, preferred_element_type=jnp.float32)
    d_mixed = jnp.dot(d_resid_bf, back_proj.T, preferred_element_type=jnp.float32)
    d_mixed = d_mixed.astype(jnp.bfloat16).reshape(batch, length, H, head_size)
    scores_again = product('bqhd,bkhd->bhqk', query, key_arr) * scale
    probs_full = jnp.exp(scores_again - log_total)
    probs_again = probs_full.astype(jnp.bfloat16)
    d_probs = product('bqhd,bkhd->bhqk', d_mixed, value)
    d_value = product('bhqk,bqhd->bkhd', probs_again, d_mixed).reshape(token_rows, width)
    delta = lax.optimization_barrier(jnp.sum(probs_full * d_probs, -1, keepdims=True))
    d_scores = (probs_full * (d_probs - delta) * scale).astype(jnp.bfloat16)
    d_query = product('bhqk,bkhd->bqhd', d_scores, key_arr).reshape(token_rows, width)
    d_key = product('bhqk,bqhd->bkhd', d_scores, query).reshape(token_rows, width)
    grad_qbias = lax.optimization_barrier(jnp.sum(d_query, 0))
    grad_vbias = lax.optimization_barrier(jnp.sum(d_value, 0))
    d_qkv = jnp.concatenate([d_query, d_key, d_value], 1).astype(jnp.bfloat16)
    grad_qkv = jnp.dot(first_normed_rows.T, d_qkv, preferred_element_type=jnp.float32)
    first_norm_gradient = jnp.dot(d_qkv, back_qkv.T, preferred_element_type=jnp.float32)
    gain1_gradient = lax.optimization_barrier(jnp.sum(first_norm_gradient * first_centered_scaled, 0))
    grad_shift1 = lax.optimization_barrier(jnp.sum(first_norm_gradient, 0))
    input_gradient = residual_gradient + layer_norm_backward(first_norm_gradient * backward_vector_slice[0], first_centered_scaled, first_inverse_deviation)
    grad_vectors = jnp.stack([gain1_gradient, grad_shift1, grad_qbias, grad_vbias, grad_pbias, gain2_gradient, grad_shift2, grad_bias2])
    grads = (grad_qkv, grad_proj, grad_fc1, grad_fc2, grad_vectors, grad_bias1)
    out_block = result.astype(jnp.bfloat16).reshape(batch, length, width)
    input_block = input_gradient.astype(jnp.bfloat16).reshape(batch, length, width)
    return (out_block, input_block, grads)

def adamw(weight_vals, grad_vals, first_vals, second_vals):
    first_new = beta_one * first_vals + (1.0 - beta_one) * grad_vals
    second_new = beta_two * second_vals + (1.0 - beta_two) * grad_vals * grad_vals
    first_hat = first_new / (1.0 - beta_one ** 2)
    second_hat = second_new / (1.0 - beta_two ** 2)
    updated = weight_vals - learn_rate * (first_hat / (jnp.sqrt(second_hat) + adam_eps) + decay_rate * weight_vals)
    return (updated, first_new, second_new)

def reference(images, cotangent, weights, first_moment, second_moment):
    params = unpack(weights.astype(jnp.bfloat16))
    block_size = math.gcd(IMAGES, 16)
    block_count = IMAGES // block_size
    image_blocks = images.reshape(block_count, block_size, SEQ, D)
    cot_blocks = cotangent.reshape(block_count, block_size, SEQ, D)
    initial = (jnp.zeros((D, 3 * D), jnp.float32), jnp.zeros((D, D), jnp.float32), jnp.zeros((D, FF), jnp.float32), jnp.zeros((FF, D), jnp.float32), jnp.zeros((8, D), jnp.float32), jnp.zeros((FF,), jnp.float32))

    def advance(carry, blocks):
        out_block, input_block, grads = layer_block(blocks[0], blocks[1], params, params)
        summed = jax.tree.map(lambda older, newer: older + newer, carry, grads)
        return (summed, (out_block, input_block))
    grads, (outs, input_grads) = lax.scan(advance, initial, (image_blocks, cot_blocks))
    flat_grad = pack(grads, FLAT)
    new_weights, new_first, new_second = adamw(weights, flat_grad, first_moment, second_moment)
    return (outs.reshape(IMAGES, SEQ, D), input_grads.reshape(IMAGES, SEQ, D), new_weights, flat_grad, new_first, new_second)
```

```python
import functools

import jax
import jax.numpy as jnp
from jax import lax
from jax.experimental import pallas as pl
from jax.experimental.pallas import tpu as pltpu
from jax.sharding import PartitionSpec as P

D = 384
H = 6
FF = 1536
LANES = 128

norm_eps = 1e-06
half_root = 0.7071067811865476
inv_root_two_pi = 0.3989422804014327
beta_one = 0.9
beta_two = 0.999
learn_rate = 0.02
decay_rate = 0.05
adam_eps = 1e-08

AT_QKV = 0
AT_PROJ = AT_QKV + 3 * D * D // LANES
AT_FC1 = AT_PROJ + D * D // LANES
AT_FC2 = AT_FC1 + D * FF // LANES
AT_VEC = AT_FC2 + FF * D // LANES
AT_B1 = AT_VEC + 8 * D // LANES
AT_TAIL = AT_B1 + FF // LANES

BF = jnp.bfloat16
F32 = jnp.float32


def nn(a, b):
    return lax.dot_general(a, b, (((1,), (0,)), ((), ())), preferred_element_type=F32)


def nt(a, b):
    return lax.dot_general(a, b, (((1,), (1,)), ((), ())), preferred_element_type=F32)


def tn(a, b):
    return lax.dot_general(a, b, (((0,), (0,)), ((), ())), preferred_element_type=F32)


def normalize(values):
    centred = values - jnp.mean(values, -1, keepdims=True)
    inverse = lax.rsqrt(jnp.mean(centred * centred, -1, keepdims=True) + norm_eps)
    return centred * inverse, inverse


def normalize_back(d_scaled, scaled, inverse):
    first_mean = jnp.mean(d_scaled, -1, keepdims=True)
    second_mean = jnp.mean(d_scaled * scaled, -1, keepdims=True)
    return (d_scaled - first_mean - scaled * second_mean) * inverse


def columns(x):
    return jnp.sum(x, 0, keepdims=True)


def unpack_into(flat, wq, wp, w1, w2, vec, b1):
    for ref, base in ((wq, AT_QKV), (wp, AT_PROJ), (w1, AT_FC1), (w2, AT_FC2)):
        rows, blocks = ref.shape[0], ref.shape[1] // LANES
        for j in range(blocks):
            ref[:, j * LANES : (j + 1) * LANES] = flat[pl.ds(base + j, rows, stride=blocks), :].astype(BF)
    for c in range(D // LANES):
        vec[:, c * LANES : (c + 1) * LANES] = flat[pl.ds(AT_VEC + c, 8, stride=D // LANES), :]
    for c in range(FF // LANES):
        b1[:, c * LANES : (c + 1) * LANES] = flat[AT_B1 + c : AT_B1 + c + 1, :]


def pack_into(flat, aq, ap, a1, a2, avec, ab1):
    for ref, base in ((aq, AT_QKV), (ap, AT_PROJ), (a1, AT_FC1), (a2, AT_FC2)):
        rows, blocks = ref.shape[0], ref.shape[1] // LANES
        for j in range(blocks):
            flat[pl.ds(base + j, rows, stride=blocks), :] = ref[:, j * LANES : (j + 1) * LANES]
    for c in range(D // LANES):
        flat[pl.ds(AT_VEC + c, 8, stride=D // LANES), :] = avec[:, c * LANES : (c + 1) * LANES]
    for c in range(FF // LANES):
        flat[AT_B1 + c : AT_B1 + c + 1, :] = ab1[:, c * LANES : (c + 1) * LANES]
    flat[AT_TAIL:, :] = jnp.zeros((flat.shape[0] - AT_TAIL, LANES), F32)


def image_step(seq, img, cot, out, dinp, wq, wp, w1, w2, vec, b1, aq, ap, a1, a2, avec, ab1, xs, gs, pf):
    pad = xs.shape[0]
    xs[0:seq, :] = img[0].astype(F32)
    gs[0:seq, :] = cot[0].astype(F32)
    x = xs[...]
    xhat1, inv1 = normalize(x)
    normed1 = (xhat1 * vec[0:1, :] + vec[1:2, :]).astype(BF)
    q = (nn(normed1, wq[:, :D]) + vec[2:3, :]).astype(BF)
    k = nn(normed1, wq[:, D : 2 * D]).astype(BF)
    v = (nn(normed1, wq[:, 2 * D :]) + vec[3:4, :]).astype(BF)
    scale = (D // H) ** (-0.5)
    lane = lax.broadcasted_iota(jnp.int32, (1, LANES), 1)
    halves = [(lane < 64), (lane >= 64)]
    key_ok = lax.broadcasted_iota(jnp.int32, (1, pad), 1) < seq

    def half(block, i):
        return jnp.where(halves[i], block, jnp.zeros_like(block))

    mixed_blocks = []
    for pair in range(D // LANES):
        cut = slice(pair * LANES, (pair + 1) * LANES)
        total = None
        for i in range(2):
            s = nt(half(q[:, cut], i), k[:, cut]) * scale
            s = jnp.where(key_ok, s, -1e30)
            e = jnp.exp(s - jnp.max(s, -1, keepdims=True))
            p = e * (1.0 / jnp.sum(e, -1, keepdims=True))
            pf[2 * pair + i] = p
            term = nn(p.astype(BF), half(v[:, cut], i))
            total = term if total is None else total + term
        mixed_blocks.append(total.astype(BF))
    mixed = jnp.concatenate(mixed_blocks, 1)
    resid = x + nn(mixed, wp[...]) + vec[4:5, :]
    xhat2, inv2 = normalize(resid)
    normed2 = (xhat2 * vec[5:6, :] + vec[6:7, :]).astype(BF)
    dout_f = gs[...]
    dout = dout_f.astype(BF)
    result = resid + vec[7:8, :]
    dnorm2 = None
    step = 512
    for c in range(0, FF, step):
        cut = slice(c, c + step)
        pre = nn(normed2, w1[:, cut]) + b1[:, cut]
        cdf = 0.5 * (1.0 + lax.erf(pre * half_root))
        act = (pre * cdf).astype(BF)
        result = result + nn(act, w2[cut, :])
        a2[cut, :] += tn(act, dout)
        dact = nt(dout, w2[cut, :])
        dpre = dact * (cdf + pre * jnp.exp(-0.5 * pre * pre) * inv_root_two_pi)
        ab1[:, cut] += columns(dpre)
        dpre_b = dpre.astype(BF)
        a1[:, cut] += tn(normed2, dpre_b)
        term = nt(dpre_b, w1[:, cut])
        dnorm2 = term if dnorm2 is None else dnorm2 + term
    out[0] = result.astype(BF)[0:seq, :]
    avec[7:8, :] += columns(dout_f)
    avec[5:6, :] += columns(dnorm2 * xhat2)
    avec[6:7, :] += columns(dnorm2)
    dresid = dout_f + normalize_back(dnorm2 * vec[5:6, :], xhat2, inv2)
    avec[4:5, :] += columns(dresid)
    dresid_b = dresid.astype(BF)
    ap[...] += tn(mixed, dresid_b)
    dmixed = nt(dresid_b, wp[...]).astype(BF)
    dq_blocks, dk_blocks, dv_blocks = [], [], []
    for pair in range(D // LANES):
        cut = slice(pair * LANES, (pair + 1) * LANES)
        dq = dk = dv = None
        for i in range(2):
            p = pf[2 * pair + i]
            dm = half(dmixed[:, cut], i)
            dp = nt(dm, v[:, cut])
            delta = jnp.sum(p * dp, -1, keepdims=True)
            ds = (p * (dp - delta) * scale).astype(BF)
            terms = (
                nn(ds, half(k[:, cut], i)),
                tn(ds, half(q[:, cut], i)),
                tn(p.astype(BF), dm),
            )
            if dq is None:
                dq, dk, dv = terms
            else:
                dq, dk, dv = dq + terms[0], dk + terms[1], dv + terms[2]
        avec[2:3, cut] += columns(dq)
        avec[3:4, cut] += columns(dv)
        dq_blocks.append(dq.astype(BF))
        dk_blocks.append(dk.astype(BF))
        dv_blocks.append(dv.astype(BF))
    dnorm1 = None
    for part, blocks in enumerate((dq_blocks, dk_blocks, dv_blocks)):
        cut = slice(part * D, (part + 1) * D)
        d_part = jnp.concatenate(blocks, 1)
        aq[:, cut] += tn(normed1, d_part)
        term = nt(d_part, wq[:, cut])
        dnorm1 = term if dnorm1 is None else dnorm1 + term
    avec[0:1, :] += columns(dnorm1 * xhat1)
    avec[1:2, :] += columns(dnorm1)
    dx = dresid + normalize_back(dnorm1 * vec[0:1, :], xhat1, inv1)
    dinp[0] = dx.astype(BF)[0:seq, :]


def compute_kernel(seq, img, cot, pflat, out, dinp, gflat, wq, wp, w1, w2, vec, b1, aq, ap, a1, a2, avec, ab1, xs, gs, pf):
    @pl.when(pl.program_id(0) == 0)
    def _():
        gflat[...] = pflat[...].astype(F32)
        unpack_into(gflat, wq, wp, w1, w2, vec, b1)
        for ref in (aq, ap, a1, a2, avec, ab1, xs, gs):
            ref[...] = jnp.zeros_like(ref)

    image_step(seq, img, cot, out, dinp, wq, wp, w1, w2, vec, b1, aq, ap, a1, a2, avec, ab1, xs, gs, pf)

    @pl.when(pl.program_id(0) == pl.num_programs(0) - 1)
    def _():
        pack_into(gflat, aq, ap, a1, a2, avec, ab1)


def compute(images, cotangent, params):
    batch, seq, width = images.shape
    pad = (seq + 15) // 16 * 16
    rows = params.shape[0]
    per_image = pl.BlockSpec((1, seq, width), lambda i: (i, 0, 0))
    whole = pl.BlockSpec(memory_space=pltpu.VMEM)
    mats = [(D, 3 * D), (D, D), (D, FF), (FF, D)]
    vecs = [(8, D), (1, FF)]
    return pl.pallas_call(
        functools.partial(compute_kernel, seq),
        grid=(batch,),
        in_specs=[per_image, per_image, whole],
        out_specs=[per_image, per_image, whole],
        out_shape=[
            jax.ShapeDtypeStruct(images.shape, BF),
            jax.ShapeDtypeStruct(images.shape, BF),
            jax.ShapeDtypeStruct((rows, LANES), F32),
        ],
        scratch_shapes=[pltpu.VMEM(s, BF) for s in mats]
        + [pltpu.VMEM(s, F32) for s in vecs]
        + [pltpu.VMEM(s, F32) for s in mats + vecs]
        + [pltpu.VMEM((pad, width), F32)] * 2
        + [pltpu.VMEM((H, pad, pad), F32)],
        compiler_params=pltpu.CompilerParams(vmem_limit_bytes=60 * 2**20),
    )(images, cotangent, params)


def adamw(weight_vals, grad_vals, first_vals, second_vals):
    first_new = beta_one * first_vals + (1.0 - beta_one) * grad_vals
    second_new = beta_two * second_vals + (1.0 - beta_two) * grad_vals * grad_vals
    first_hat = first_new / (1.0 - beta_one**2)
    second_hat = second_new / (1.0 - beta_two**2)
    change = -learn_rate * (first_hat / (jnp.sqrt(second_hat) + adam_eps) + decay_rate * weight_vals)
    return (change, first_new, second_new)


def on_device(images, cotangent, weights, first_moment, second_moment):
    half_bf = weights.astype(BF)
    params = lax.all_gather(half_bf, "fsdp", axis=0, tiled=True).reshape(-1, LANES)
    output, input_grad, flat_grad = compute(images, cotangent, params)
    own_grad = lax.psum_scatter(
        flat_grad.reshape(-1).astype(BF), ("fsdp", "rep"), scatter_dimension=0, tiled=True
    ).astype(F32)
    piece_len = first_moment.shape[0]
    offset = lax.axis_index("rep") * piece_len
    own_weights = lax.dynamic_slice_in_dim(weights, offset, piece_len)
    change, new_first, new_second = adamw(own_weights, own_grad, first_moment, second_moment)
    changes = lax.all_gather(change.astype(BF), "rep", axis=0, tiled=True)
    new_weights = weights + changes.astype(F32)
    return (output, input_grad, new_weights, own_grad, new_first, new_second)


def solution(mesh):
    in_specs = (
        P(("fsdp", "rep"), None, None),
        P(("fsdp", "rep"), None, None),
        P("fsdp"),
        P(("fsdp", "rep")),
        P(("fsdp", "rep")),
    )
    out_specs = (
        P(("fsdp", "rep"), None, None),
        P(("fsdp", "rep"), None, None),
        P("fsdp"),
        P(("fsdp", "rep")),
        P(("fsdp", "rep")),
        P(("fsdp", "rep")),
    )
    return jax.shard_map(
        on_device, mesh=mesh, in_specs=in_specs, out_specs=out_specs, check_vma=False
    )
```

```python
import functools

import jax
import jax.numpy as jnp
from jax import lax
from jax.experimental import pallas as pl
from jax.experimental.pallas import tpu as pltpu
from jax.sharding import PartitionSpec as P

D = 384
H = 6
FF = 1536
LANES = 128

norm_eps = 1e-06
half_root = 0.7071067811865476
inv_root_two_pi = 0.3989422804014327
beta_one = 0.9
beta_two = 0.999
learn_rate = 0.02
decay_rate = 0.05
adam_eps = 1e-08

AT_QKV = 0
AT_PROJ = AT_QKV + 3 * D * D // LANES
AT_FC1 = AT_PROJ + D * D // LANES
AT_FC2 = AT_FC1 + D * FF // LANES
AT_VEC = AT_FC2 + FF * D // LANES
AT_B1 = AT_VEC + 8 * D // LANES
AT_TAIL = AT_B1 + FF // LANES

BF = jnp.bfloat16
F32 = jnp.float32


def nn(a, b):
    return lax.dot_general(a, b, (((1,), (0,)), ((), ())), preferred_element_type=F32)


def nt(a, b):
    return lax.dot_general(a, b, (((1,), (1,)), ((), ())), preferred_element_type=F32)


def tn(a, b):
    return lax.dot_general(a, b, (((0,), (0,)), ((), ())), preferred_element_type=F32)


def normalize(values):
    centred = values - jnp.mean(values, -1, keepdims=True)
    inverse = lax.rsqrt(jnp.mean(centred * centred, -1, keepdims=True) + norm_eps)
    return centred * inverse, inverse


def normalize_back(d_scaled, scaled, inverse):
    first_mean = jnp.mean(d_scaled, -1, keepdims=True)
    second_mean = jnp.mean(d_scaled * scaled, -1, keepdims=True)
    return (d_scaled - first_mean - scaled * second_mean) * inverse


def columns(x):
    return jnp.sum(x, 0, keepdims=True)


def unpack_into(flat, wq, wp, w1, w2, vec, b1):
    for ref, base in ((wq, AT_QKV), (wp, AT_PROJ), (w1, AT_FC1), (w2, AT_FC2)):
        rows, blocks = ref.shape[0], ref.shape[1] // LANES
        for j in range(blocks):
            ref[:, j * LANES : (j + 1) * LANES] = flat[pl.ds(base + j, rows, stride=blocks), :].astype(BF)
    for c in range(D // LANES):
        vec[:, c * LANES : (c + 1) * LANES] = flat[pl.ds(AT_VEC + c, 8, stride=D // LANES), :]
    for c in range(FF // LANES):
        b1[:, c * LANES : (c + 1) * LANES] = flat[AT_B1 + c : AT_B1 + c + 1, :]


def pack_into(flat, aq, ap, a1, a2, avec, ab1):
    for ref, base in ((aq, AT_QKV), (ap, AT_PROJ), (a1, AT_FC1), (a2, AT_FC2)):
        rows, blocks = ref.shape[0], ref.shape[1] // LANES
        for j in range(blocks):
            flat[pl.ds(base + j, rows, stride=blocks), :] = ref[:, j * LANES : (j + 1) * LANES]
    for c in range(D // LANES):
        flat[pl.ds(AT_VEC + c, 8, stride=D // LANES), :] = avec[:, c * LANES : (c + 1) * LANES]
    for c in range(FF // LANES):
        flat[AT_B1 + c : AT_B1 + c + 1, :] = ab1[:, c * LANES : (c + 1) * LANES]
    flat[AT_TAIL:, :] = jnp.zeros((flat.shape[0] - AT_TAIL, LANES), F32)


def image_step(seq, img, cot, out, dinp, wq, wp, w1, w2, vec, b1, aq, ap, a1, a2, avec, ab1, xs, gs, pf):
    pad = xs.shape[0]
    xs[0:seq, :] = img[0].astype(F32)
    gs[0:seq, :] = cot[0].astype(F32)
    x = xs[...]
    xhat1, inv1 = normalize(x)
    normed1 = (xhat1 * vec[0:1, :] + vec[1:2, :]).astype(BF)
    q = (nn(normed1, wq[:, :D]) + vec[2:3, :]).astype(BF)
    k = nn(normed1, wq[:, D : 2 * D]).astype(BF)
    v = (nn(normed1, wq[:, 2 * D :]) + vec[3:4, :]).astype(BF)
    scale = (D // H) ** (-0.5)
    lane = lax.broadcasted_iota(jnp.int32, (1, LANES), 1)
    halves = [(lane < 64), (lane >= 64)]
    key_ok = lax.broadcasted_iota(jnp.int32, (1, pad), 1) < seq

    def half(block, i):
        return jnp.where(halves[i], block, jnp.zeros_like(block))

    mixed_blocks = []
    for pair in range(D // LANES):
        cut = slice(pair * LANES, (pair + 1) * LANES)
        total = None
        for i in range(2):
            s = nt(half(q[:, cut], i), k[:, cut]) * scale
            s = jnp.where(key_ok, s, -1e30)
            e = jnp.exp(s - jnp.max(s, -1, keepdims=True))
            p = e * (1.0 / jnp.sum(e, -1, keepdims=True))
            pf[2 * pair + i] = p
            term = nn(p.astype(BF), half(v[:, cut], i))
            total = term if total is None else total + term
        mixed_blocks.append(total.astype(BF))
    mixed = jnp.concatenate(mixed_blocks, 1)
    resid = x + nn(mixed, wp[...]) + vec[4:5, :]
    xhat2, inv2 = normalize(resid)
    normed2 = (xhat2 * vec[5:6, :] + vec[6:7, :]).astype(BF)
    dout_f = gs[...]
    dout = dout_f.astype(BF)
    result = resid + vec[7:8, :]
    dnorm2 = None
    step = 512
    for c in range(0, FF, step):
        cut = slice(c, c + step)
        pre = nn(normed2, w1[:, cut]) + b1[:, cut]
        cdf = 0.5 * (1.0 + lax.erf(pre * half_root))
        act = (pre * cdf).astype(BF)
        result = result + nn(act, w2[cut, :])
        a2[cut, :] += tn(act, dout)
        dact = nt(dout, w2[cut, :])
        dpre = dact * (cdf + pre * jnp.exp(-0.5 * pre * pre) * inv_root_two_pi)
        ab1[:, cut] += columns(dpre)
        dpre_b = dpre.astype(BF)
        a1[:, cut] += tn(normed2, dpre_b)
        term = nt(dpre_b, w1[:, cut])
        dnorm2 = term if dnorm2 is None else dnorm2 + term
    out[0] = result.astype(BF)[0:seq, :]
    avec[7:8, :] += columns(dout_f)
    avec[5:6, :] += columns(dnorm2 * xhat2)
    avec[6:7, :] += columns(dnorm2)
    dresid = dout_f + normalize_back(dnorm2 * vec[5:6, :], xhat2, inv2)
    avec[4:5, :] += columns(dresid)
    dresid_b = dresid.astype(BF)
    ap[...] += tn(mixed, dresid_b)
    dmixed = nt(dresid_b, wp[...]).astype(BF)
    dq_blocks, dk_blocks, dv_blocks = [], [], []
    for pair in range(D // LANES):
        cut = slice(pair * LANES, (pair + 1) * LANES)
        dq = dk = dv = None
        for i in range(2):
            p = pf[2 * pair + i]
            dm = half(dmixed[:, cut], i)
            dp = nt(dm, v[:, cut])
            delta = jnp.sum(p * dp, -1, keepdims=True)
            ds = (p * (dp - delta) * scale).astype(BF)
            terms = (
                nn(ds, half(k[:, cut], i)),
                tn(ds, half(q[:, cut], i)),
                tn(p.astype(BF), dm),
            )
            if dq is None:
                dq, dk, dv = terms
            else:
                dq, dk, dv = dq + terms[0], dk + terms[1], dv + terms[2]
        avec[2:3, cut] += columns(dq)
        avec[3:4, cut] += columns(dv)
        dq_blocks.append(dq.astype(BF))
        dk_blocks.append(dk.astype(BF))
        dv_blocks.append(dv.astype(BF))
    dnorm1 = None
    for part, blocks in enumerate((dq_blocks, dk_blocks, dv_blocks)):
        cut = slice(part * D, (part + 1) * D)
        d_part = jnp.concatenate(blocks, 1)
        aq[:, cut] += tn(normed1, d_part)
        term = nt(d_part, wq[:, cut])
        dnorm1 = term if dnorm1 is None else dnorm1 + term
    avec[0:1, :] += columns(dnorm1 * xhat1)
    avec[1:2, :] += columns(dnorm1)
    dx = dresid + normalize_back(dnorm1 * vec[0:1, :], xhat1, inv1)
    dinp[0] = dx.astype(BF)[0:seq, :]


def compute_kernel(seq, img, cot, pflat, out, dinp, gflat, wq, wp, w1, w2, vec, b1, aq, ap, a1, a2, avec, ab1, xs, gs, pf):
    @pl.when(pl.program_id(0) == 0)
    def _():
        gflat[...] = pflat[...].astype(F32)
        unpack_into(gflat, wq, wp, w1, w2, vec, b1)
        for ref in (aq, ap, a1, a2, avec, ab1, xs, gs):
            ref[...] = jnp.zeros_like(ref)

    image_step(seq, img, cot, out, dinp, wq, wp, w1, w2, vec, b1, aq, ap, a1, a2, avec, ab1, xs, gs, pf)

    @pl.when(pl.program_id(0) == pl.num_programs(0) - 1)
    def _():
        pack_into(gflat, aq, ap, a1, a2, avec, ab1)


def compute(images, cotangent, params):
    batch, seq, width = images.shape
    pad = (seq + 15) // 16 * 16
    rows = params.shape[0]
    per_image = pl.BlockSpec((1, seq, width), lambda i: (i, 0, 0))
    whole = pl.BlockSpec(memory_space=pltpu.VMEM)
    mats = [(D, 3 * D), (D, D), (D, FF), (FF, D)]
    vecs = [(8, D), (1, FF)]
    return pl.pallas_call(
        functools.partial(compute_kernel, seq),
        grid=(batch,),
        in_specs=[per_image, per_image, whole],
        out_specs=[per_image, per_image, whole],
        out_shape=[
            jax.ShapeDtypeStruct(images.shape, BF),
            jax.ShapeDtypeStruct(images.shape, BF),
            jax.ShapeDtypeStruct((rows, LANES), F32),
        ],
        scratch_shapes=[pltpu.VMEM(s, BF) for s in mats]
        + [pltpu.VMEM(s, F32) for s in vecs]
        + [pltpu.VMEM(s, F32) for s in mats + vecs]
        + [pltpu.VMEM((pad, width), F32)] * 2
        + [pltpu.VMEM((H, pad, pad), F32)],
        compiler_params=pltpu.CompilerParams(vmem_limit_bytes=60 * 2**20),
    )(images, cotangent, params)


MESH = pl.DeviceIdType.MESH


def place():
    f, r = lax.axis_index("fsdp"), lax.axis_index("rep")

    def across(bit):
        return r + bit * (1 - 2 * ((r // bit) % 2))

    return f, r, across


def greet(partners):
    barrier = pltpu.get_barrier_semaphore()
    for partner in partners:
        pl.semaphore_signal(barrier, inc=1, device_id=partner, device_id_type=MESH)
    pl.semaphore_wait(barrier, len(partners))


def gather_kernel(steps, half, out, local_sem, send_sem, recv_sem):
    f, r, across = place()
    c, y = r % 2, (r // 2) % 2
    peer, side, core = (1 - f, r), (f, across(2)), (f, across(1))
    greet([peer, side, core])
    mine = (2 * y + c) * steps
    sides = (2 * (1 - y) + c) * steps

    def copy(src, dst, kind, s, to):
        return pltpu.make_async_remote_copy(
            src_ref=src, dst_ref=dst, send_sem=send_sem.at[kind, s], recv_sem=recv_sem.at[kind, s],
            device_id=to, device_id_type=MESH,
        )

    first = [copy(half.at[mine + s], out.at[f, mine + s], 0, s, peer) for s in range(steps)]
    for one in first:
        one.start()
    own = pltpu.make_async_copy(half, out.at[f], local_sem)
    own.start()

    def relay(kind, s, base, to):
        ref = out.at[1 - f, base + s]
        return copy(ref, ref, kind, s, to)

    second = [relay(1, s, mine, side) for s in range(steps)]
    third = [relay(2, s, mine, core) for s in range(steps)]
    fourth = [relay(3, s, sides, core) for s in range(steps)]
    for s in range(steps):
        first[s].wait_recv()
        second[s].start()
        third[s].start()
    for s in range(steps):
        second[s].wait_recv()
        fourth[s].start()
    for s in range(steps):
        third[s].wait_recv()
        fourth[s].wait_recv()
    for group in (first, second, third, fourth):
        for one in group:
            one.wait_send()
    own.wait()


def gather_params(half_bf):
    rows = half_bf.shape[0] // LANES
    quarter = rows // 4
    steps = next(s for s in (7, 5, 4, 3, 2, 1) if quarter % (8 * s) == 0)
    shape = (4 * steps, quarter // steps, LANES)
    out = pl.pallas_call(
        functools.partial(gather_kernel, steps),
        in_specs=[pl.BlockSpec(memory_space=pltpu.VMEM)],
        out_specs=pl.BlockSpec(memory_space=pltpu.VMEM),
        out_shape=jax.ShapeDtypeStruct((2,) + shape, BF),
        scratch_shapes=[
            pltpu.SemaphoreType.DMA,
            pltpu.SemaphoreType.DMA((4, steps)),
            pltpu.SemaphoreType.DMA((4, steps)),
        ],
        compiler_params=pltpu.CompilerParams(collective_id=0, has_side_effects=True),
    )(half_bf.reshape(shape))
    return out.reshape(2 * rows, LANES)


def orders(bits):
    rest = [b for b in bits if b > 1]
    low, high = rest[:2], rest[2:]
    dims = [0] + low
    return [[1] + dims[i:] + dims[:i] + high for i in range(len(dims))]


def reduce_kernel(reps, size, flat, weights, m_in, v_in, new_w, grad, m_out, v_out, acc, sbuf, rbuf, ag, s_send, s_recv, a_send, a_recv):
    f, r, across = place()
    bits = [1 << i for i in range(reps.bit_length() - 1)]
    plans = orders(bits)
    parts, rows = acc.shape[1], acc.shape[2]

    def bit_of(dim):
        return f if dim == 0 else (r // dim) % 2

    def stride(dim):
        return reps if dim == 0 else dim

    def partner(dim):
        return (1 - f, r) if dim == 0 else (f, across(dim))

    greet([partner(dim) for dim in [0] + bits])

    spans = [(k * rows, min((k + 1) * rows, size)) for k in range(parts)]
    for p in range(2 * reps):
        for k, (lo, hi) in enumerate(spans):
            if hi < lo + rows:
                acc[p, k] = jnp.zeros((rows, LANES), F32)
            acc[p, k, 0 : hi - lo, :] = flat[p * size + lo : p * size + hi, :]

    def members(fixed, free):
        base = sum(value * stride(dim) for dim, value in fixed)
        out = [base]
        for dim in free:
            out = [i + v * stride(dim) for i in out for v in (0, 1)]
        return out

    pending = {}
    offsets = [0] * parts
    depth = len(bits) + 1
    for stage in range(depth):
        for k in range(parts):
            plan = plans[k]
            dim, free = plan[stage], plan[stage + 1 :]
            settled = [(d, bit_of(d)) for d in plan[:stage]]
            if stage:
                copy, old, count = pending[k]
                copy.wait_recv()
                for j, i in enumerate(members(settled, plan[stage:])):
                    acc[i, k] += rbuf[k, old + j].astype(F32)
            count = 1 << len(free)
            start = offsets[k]
            for j, i in enumerate(members(settled + [(dim, 1 - bit_of(dim))], free)):
                sbuf[k, start + j] = acc[i, k].astype(BF)
            copy = pltpu.make_async_remote_copy(
                src_ref=sbuf.at[k, pl.ds(start, count)], dst_ref=rbuf.at[k, pl.ds(start, count)],
                send_sem=s_send.at[k, stage], recv_sem=s_recv.at[k, stage],
                device_id=partner(dim), device_id_type=MESH,
            )
            copy.start()
            pending.setdefault("all", []).append(copy)
            pending[k] = (copy, start, count)
            offsets[k] = start + count

    me = f * reps + r
    waits = []
    for k in range(parts):
        copy, old, count = pending[k]
        copy.wait_recv()
        lo, hi = spans[k]
        n = hi - lo
        g = (acc[me, k] + rbuf[k, old].astype(F32))[:n]
        grad[lo:hi, :] = g
        first = beta_one * m_in[lo:hi, :] + (1.0 - beta_one) * g
        second = beta_two * v_in[lo:hi, :] + (1.0 - beta_two) * g * g
        m_out[lo:hi, :] = first
        v_out[lo:hi, :] = second
        w = weights[pl.ds(r * size + lo, n), :]
        first_hat = first * (1.0 / (1.0 - beta_one**2))
        second_hat = second * (1.0 / (1.0 - beta_two**2))
        change = -learn_rate * (first_hat / (jnp.sqrt(second_hat) + adam_eps) + decay_rate * w)
        if n < rows:
            ag[r, k] = jnp.zeros((rows, LANES), BF)
        ag[r, k, 0:n, :] = change.astype(BF)

    def spread(k, stage):
        plan = [d for d in plans[k] if d > 0][::-1]
        dim = plan[stage]
        fixed = [(d, bit_of(d)) for d in plan[stage:]]
        copies = []
        for j, i in enumerate(members(fixed, plan[:stage])):
            ref = ag.at[i, k]
            at = (1 << stage) - 1 + j
            copies.append(
                pltpu.make_async_remote_copy(
                    src_ref=ref, dst_ref=ref, send_sem=a_send.at[k, at], recv_sem=a_recv.at[k, at],
                    device_id=partner(dim), device_id_type=MESH,
                )
            )
        return copies

    last = {k: [] for k in range(parts)}
    for stage in range(len(bits)):
        for k in range(parts):
            for one in last[k]:
                one.wait_recv()
            last[k] = spread(k, stage)
            for one in last[k]:
                one.start()
            waits += last[k]
    for k in range(parts):
        for one in last[k]:
            one.wait_recv()
    for p in range(reps):
        for k, (lo, hi) in enumerate(spans):
            at = slice(p * size + lo, p * size + hi)
            new_w[at, :] = weights[at, :] + ag[p, k][: hi - lo].astype(F32)
    for one in waits + pending["all"]:
        one.wait_send()


def reduce_update(flat, weights, first_moment, second_moment, reps):
    size = first_moment.shape[0] // LANES
    bits = [1 << i for i in range(reps.bit_length() - 1)]
    parts = len(orders(bits))
    rows = -(-size // (8 * parts)) * 8
    piece = jax.ShapeDtypeStruct((size, LANES), F32)
    stages = len(bits) + 1
    outs = pl.pallas_call(
        functools.partial(reduce_kernel, reps, size),
        in_specs=[pl.BlockSpec(memory_space=pltpu.VMEM)] * 4,
        out_specs=[pl.BlockSpec(memory_space=pltpu.VMEM)] * 4,
        out_shape=[jax.ShapeDtypeStruct((reps * size, LANES), F32), piece, piece, piece],
        scratch_shapes=[
            pltpu.VMEM((2 * reps, parts, rows, LANES), F32),
            pltpu.VMEM((parts, 2 * reps - 1, rows, LANES), BF),
            pltpu.VMEM((parts, 2 * reps - 1, rows, LANES), BF),
            pltpu.VMEM((reps, parts, rows, LANES), BF),
            pltpu.SemaphoreType.DMA((parts, stages)),
            pltpu.SemaphoreType.DMA((parts, stages)),
            pltpu.SemaphoreType.DMA((parts, reps)),
            pltpu.SemaphoreType.DMA((parts, reps)),
        ],
        compiler_params=pltpu.CompilerParams(
            collective_id=1, has_side_effects=True, vmem_limit_bytes=60 * 2**20
        ),
    )(flat, weights.reshape(-1, LANES), first_moment.reshape(-1, LANES), second_moment.reshape(-1, LANES))
    return [o.reshape(-1) for o in outs]


def on_device(reps, images, cotangent, weights, first_moment, second_moment):
    params = gather_params(weights.astype(BF))
    output, input_grad, flat_grad = compute(images, cotangent, params)
    new_weights, own_grad, new_first, new_second = reduce_update(
        flat_grad, weights, first_moment, second_moment, reps
    )
    return (output, input_grad, new_weights, own_grad, new_first, new_second)


def solution(mesh):
    in_specs = (
        P(("fsdp", "rep"), None, None),
        P(("fsdp", "rep"), None, None),
        P("fsdp"),
        P(("fsdp", "rep")),
        P(("fsdp", "rep")),
    )
    out_specs = (
        P(("fsdp", "rep"), None, None),
        P(("fsdp", "rep"), None, None),
        P("fsdp"),
        P(("fsdp", "rep")),
        P(("fsdp", "rep")),
        P(("fsdp", "rep")),
    )
    return jax.shard_map(
        functools.partial(on_device, mesh.shape["rep"]), mesh=mesh, in_specs=in_specs, out_specs=out_specs, check_vma=False
    )
```

```python
import functools

import jax
import jax.numpy as jnp
from jax import lax
from jax.experimental import pallas as pl
from jax.experimental.pallas import tpu as pltpu
from jax.sharding import PartitionSpec as P

D = 384
H = 6
FF = 1536
LANES = 128

norm_eps = 1e-06
half_root = 0.7071067811865476
inv_root_two_pi = 0.3989422804014327
beta_one = 0.9
beta_two = 0.999
learn_rate = 0.02
decay_rate = 0.05
adam_eps = 1e-08

AT_QKV = 0
AT_PROJ = AT_QKV + 3 * D * D // LANES
AT_FC1 = AT_PROJ + D * D // LANES
AT_FC2 = AT_FC1 + D * FF // LANES
AT_VEC = AT_FC2 + FF * D // LANES
AT_B1 = AT_VEC + 8 * D // LANES
AT_TAIL = AT_B1 + FF // LANES

BF = jnp.bfloat16
F32 = jnp.float32


def nn(a, b):
    return lax.dot_general(a, b, (((1,), (0,)), ((), ())), preferred_element_type=F32)


def nt(a, b):
    return lax.dot_general(a, b, (((1,), (1,)), ((), ())), preferred_element_type=F32)


def tn(a, b):
    return lax.dot_general(a, b, (((0,), (0,)), ((), ())), preferred_element_type=F32)


def normalize(values):
    centred = values - jnp.mean(values, -1, keepdims=True)
    inverse = lax.rsqrt(jnp.mean(centred * centred, -1, keepdims=True) + norm_eps)
    return centred * inverse, inverse


def normalize_back(d_scaled, scaled, inverse):
    first_mean = jnp.mean(d_scaled, -1, keepdims=True)
    second_mean = jnp.mean(d_scaled * scaled, -1, keepdims=True)
    return (d_scaled - first_mean - scaled * second_mean) * inverse


def columns(x):
    return jnp.sum(x, 0, keepdims=True)


def unpack_into(flat, wq, wp, w1, w2, vec, b1):
    for ref, base in ((wq, AT_QKV), (wp, AT_PROJ), (w1, AT_FC1), (w2, AT_FC2)):
        rows, blocks = ref.shape[0], ref.shape[1] // LANES
        for j in range(blocks):
            ref[:, j * LANES : (j + 1) * LANES] = flat[pl.ds(base + j, rows, stride=blocks), :].astype(BF)
    for c in range(D // LANES):
        vec[:, c * LANES : (c + 1) * LANES] = flat[pl.ds(AT_VEC + c, 8, stride=D // LANES), :]
    for c in range(FF // LANES):
        b1[:, c * LANES : (c + 1) * LANES] = flat[AT_B1 + c : AT_B1 + c + 1, :]


def pack_into(flat, aq, ap, a1, a2, avec, ab1):
    for ref, base in ((aq, AT_QKV), (ap, AT_PROJ), (a1, AT_FC1), (a2, AT_FC2)):
        rows, blocks = ref.shape[0], ref.shape[1] // LANES
        for j in range(blocks):
            flat[pl.ds(base + j, rows, stride=blocks), :] = ref[:, j * LANES : (j + 1) * LANES]
    for c in range(D // LANES):
        flat[pl.ds(AT_VEC + c, 8, stride=D // LANES), :] = avec[:, c * LANES : (c + 1) * LANES]
    for c in range(FF // LANES):
        flat[AT_B1 + c : AT_B1 + c + 1, :] = ab1[:, c * LANES : (c + 1) * LANES]
    flat[AT_TAIL:, :] = jnp.zeros((flat.shape[0] - AT_TAIL, LANES), F32)


def image_step(seq, img, cot, out, dinp, wq, wp, w1, w2, vec, b1, aq, ap, a1, a2, avec, ab1, xs, gs, pf):
    pad = xs.shape[0]
    xs[0:seq, :] = img[0].astype(F32)
    gs[0:seq, :] = cot[0].astype(F32)
    x = xs[...]
    xhat1, inv1 = normalize(x)
    normed1 = (xhat1 * vec[0:1, :] + vec[1:2, :]).astype(BF)
    q = (nn(normed1, wq[:, :D]) + vec[2:3, :]).astype(BF)
    k = nn(normed1, wq[:, D : 2 * D]).astype(BF)
    v = (nn(normed1, wq[:, 2 * D :]) + vec[3:4, :]).astype(BF)
    scale = (D // H) ** (-0.5)
    lane = lax.broadcasted_iota(jnp.int32, (1, LANES), 1)
    halves = [(lane < 64), (lane >= 64)]
    key_ok = lax.broadcasted_iota(jnp.int32, (1, pad), 1) < seq

    def half(block, i):
        return jnp.where(halves[i], block, jnp.zeros_like(block))

    mixed_blocks = []
    for pair in range(D // LANES):
        cut = slice(pair * LANES, (pair + 1) * LANES)
        total = None
        for i in range(2):
            s = nt(half(q[:, cut], i), k[:, cut]) * scale
            s = jnp.where(key_ok, s, -1e30)
            e = jnp.exp(s - jnp.max(s, -1, keepdims=True))
            p = e * (1.0 / jnp.sum(e, -1, keepdims=True))
            pf[2 * pair + i] = p
            term = nn(p.astype(BF), half(v[:, cut], i))
            total = term if total is None else total + term
        mixed_blocks.append(total.astype(BF))
    mixed = jnp.concatenate(mixed_blocks, 1)
    resid = x + nn(mixed, wp[...]) + vec[4:5, :]
    xhat2, inv2 = normalize(resid)
    normed2 = (xhat2 * vec[5:6, :] + vec[6:7, :]).astype(BF)
    dout_f = gs[...]
    dout = dout_f.astype(BF)
    result = resid + vec[7:8, :]
    dnorm2 = None
    step = 512
    for c in range(0, FF, step):
        cut = slice(c, c + step)
        pre = nn(normed2, w1[:, cut]) + b1[:, cut]
        cdf = 0.5 * (1.0 + lax.erf(pre * half_root))
        act = (pre * cdf).astype(BF)
        result = result + nn(act, w2[cut, :])
        a2[cut, :] += tn(act, dout)
        dact = nt(dout, w2[cut, :])
        dpre = dact * (cdf + pre * jnp.exp(-0.5 * pre * pre) * inv_root_two_pi)
        ab1[:, cut] += columns(dpre)
        dpre_b = dpre.astype(BF)
        a1[:, cut] += tn(normed2, dpre_b)
        term = nt(dpre_b, w1[:, cut])
        dnorm2 = term if dnorm2 is None else dnorm2 + term
    out[0] = result.astype(BF)[0:seq, :]
    avec[7:8, :] += columns(dout_f)
    avec[5:6, :] += columns(dnorm2 * xhat2)
    avec[6:7, :] += columns(dnorm2)
    dresid = dout_f + normalize_back(dnorm2 * vec[5:6, :], xhat2, inv2)
    avec[4:5, :] += columns(dresid)
    dresid_b = dresid.astype(BF)
    ap[...] += tn(mixed, dresid_b)
    dmixed = nt(dresid_b, wp[...]).astype(BF)
    dq_blocks, dk_blocks, dv_blocks = [], [], []
    for pair in range(D // LANES):
        cut = slice(pair * LANES, (pair + 1) * LANES)
        dq = dk = dv = None
        for i in range(2):
            p = pf[2 * pair + i]
            dm = half(dmixed[:, cut], i)
            dp = nt(dm, v[:, cut])
            delta = jnp.sum(p * dp, -1, keepdims=True)
            ds = (p * (dp - delta) * scale).astype(BF)
            terms = (
                nn(ds, half(k[:, cut], i)),
                tn(ds, half(q[:, cut], i)),
                tn(p.astype(BF), dm),
            )
            if dq is None:
                dq, dk, dv = terms
            else:
                dq, dk, dv = dq + terms[0], dk + terms[1], dv + terms[2]
        avec[2:3, cut] += columns(dq)
        avec[3:4, cut] += columns(dv)
        dq_blocks.append(dq.astype(BF))
        dk_blocks.append(dk.astype(BF))
        dv_blocks.append(dv.astype(BF))
    dnorm1 = None
    for part, blocks in enumerate((dq_blocks, dk_blocks, dv_blocks)):
        cut = slice(part * D, (part + 1) * D)
        d_part = jnp.concatenate(blocks, 1)
        aq[:, cut] += tn(normed1, d_part)
        term = nt(d_part, wq[:, cut])
        dnorm1 = term if dnorm1 is None else dnorm1 + term
    avec[0:1, :] += columns(dnorm1 * xhat1)
    avec[1:2, :] += columns(dnorm1)
    dx = dresid + normalize_back(dnorm1 * vec[0:1, :], xhat1, inv1)
    dinp[0] = dx.astype(BF)[0:seq, :]


def compute_kernel(seq, img, cot, pflat, out, dinp, gflat, wq, wp, w1, w2, vec, b1, aq, ap, a1, a2, avec, ab1, xs, gs, pf):
    @pl.when(pl.program_id(0) == 0)
    def _():
        gflat[...] = pflat[...].astype(F32)
        unpack_into(gflat, wq, wp, w1, w2, vec, b1)
        for ref in (aq, ap, a1, a2, avec, ab1, xs, gs):
            ref[...] = jnp.zeros_like(ref)

    image_step(seq, img, cot, out, dinp, wq, wp, w1, w2, vec, b1, aq, ap, a1, a2, avec, ab1, xs, gs, pf)

    @pl.when(pl.program_id(0) == pl.num_programs(0) - 1)
    def _():
        pack_into(gflat, aq, ap, a1, a2, avec, ab1)


def compute(images, cotangent, params):
    batch, seq, width = images.shape
    pad = (seq + 15) // 16 * 16
    rows = params.shape[0]
    per_image = pl.BlockSpec((1, seq, width), lambda i: (i, 0, 0))
    whole = pl.BlockSpec(memory_space=pltpu.VMEM)
    mats = [(D, 3 * D), (D, D), (D, FF), (FF, D)]
    vecs = [(8, D), (1, FF)]
    return pl.pallas_call(
        functools.partial(compute_kernel, seq),
        grid=(batch,),
        in_specs=[per_image, per_image, whole],
        out_specs=[per_image, per_image, whole],
        out_shape=[
            jax.ShapeDtypeStruct(images.shape, BF),
            jax.ShapeDtypeStruct(images.shape, BF),
            jax.ShapeDtypeStruct((rows, LANES), F32),
        ],
        scratch_shapes=[pltpu.VMEM(s, BF) for s in mats]
        + [pltpu.VMEM(s, F32) for s in vecs]
        + [pltpu.VMEM(s, F32) for s in mats + vecs]
        + [pltpu.VMEM((pad, width), F32)] * 2
        + [pltpu.VMEM((H, pad, pad), F32)],
        compiler_params=pltpu.CompilerParams(vmem_limit_bytes=36 * 2**20),
    )(images, cotangent, params)


MESH = pl.DeviceIdType.MESH


def place():
    f, r = lax.axis_index("fsdp"), lax.axis_index("rep")

    def across(bit):
        return r + bit * (1 - 2 * ((r // bit) % 2))

    return f, r, across


def greet(partners):
    barrier = pltpu.get_barrier_semaphore()
    for partner in partners:
        pl.semaphore_signal(barrier, inc=1, device_id=partner, device_id_type=MESH)
    pl.semaphore_wait(barrier, len(partners))


def gather_kernel(steps, half, out, wide, wide_sem, send_sem, recv_sem):
    f, r, across = place()
    c, y = r % 2, (r // 2) % 2
    peer, side, core = (1 - f, r), (f, across(2)), (f, across(1))
    mine = (2 * y + c) * steps
    loads = []
    for turn in range(4):
        start = ((2 * y + c + turn) % 4) * steps
        loads.append(
            pltpu.make_async_copy(
                half.at[pl.ds(start, steps)], wide.at[pl.ds(start, steps)], wide_sem.at[turn]
            )
        )
        loads[-1].start()
    greet([peer, side, core])
    sides = (2 * (1 - y) + c) * steps

    def copy(src, dst, kind, s, to):
        return pltpu.make_async_remote_copy(
            src_ref=src, dst_ref=dst, send_sem=send_sem.at[kind, s], recv_sem=recv_sem.at[kind, s],
            device_id=to, device_id_type=MESH,
        )

    first = [copy(out.at[f, mine + s], out.at[f, mine + s], 0, s, peer) for s in range(steps)]
    loads[0].wait()
    for s in range(steps):
        out[f, mine + s] = wide[mine + s].astype(BF)
        first[s].start()
    for turn in range(1, 4):
        loads[turn].wait()
        start = ((2 * y + c + turn) % 4) * steps
        for s in range(steps):
            out[f, start + s] = wide[start + s].astype(BF)

    def relay(kind, s, base, to):
        ref = out.at[1 - f, base + s]
        return copy(ref, ref, kind, s, to)

    second = [relay(1, s, mine, side) for s in range(steps)]
    third = [relay(2, s, mine, core) for s in range(steps)]
    fourth = [relay(3, s, sides, core) for s in range(steps)]
    for s in range(steps):
        first[s].wait_recv()
        second[s].start()
        third[s].start()
    for s in range(steps):
        second[s].wait_recv()
        fourth[s].start()
    for s in range(steps):
        third[s].wait_recv()
        fourth[s].wait_recv()
    for group in (first, second, third, fourth):
        for one in group:
            one.wait_send()


def gather_params(half):
    rows = half.shape[0] // LANES
    quarter = rows // 4
    steps = next(s for s in (7, 5, 4, 3, 2, 1) if quarter % (8 * s) == 0)
    shape = (4 * steps, quarter // steps, LANES)
    out = pl.pallas_call(
        functools.partial(gather_kernel, steps),
        in_specs=[pl.BlockSpec(memory_space=pl.ANY)],
        out_specs=pl.BlockSpec(memory_space=pltpu.VMEM),
        out_shape=jax.ShapeDtypeStruct((2,) + shape, BF),
        scratch_shapes=[
            pltpu.VMEM(shape, F32),
            pltpu.SemaphoreType.DMA((4,)),
            pltpu.SemaphoreType.DMA((4, steps)),
            pltpu.SemaphoreType.DMA((4, steps)),
        ],
        compiler_params=pltpu.CompilerParams(collective_id=0, has_side_effects=True, vmem_limit_bytes=16 * 2**20),
    )(half.reshape(shape))
    return out.reshape(2 * rows, LANES)


def orders(bits):
    rest = [b for b in bits if b > 1]
    low, high = rest[:2], rest[2:]
    dims = [0] + low
    return [[1] + dims[i:] + dims[:i] + high for i in range(len(dims))]


def reduce_kernel(
    reps, size, flat, weights_hbm, m_in, v_in, changes, grad, weights, acc, sbuf, rbuf, ag, w_sem, s_send, s_recv, a_send, a_recv
):
    f, r, across = place()
    bits = [1 << i for i in range(reps.bit_length() - 1)]
    plans = orders(bits)
    parts, rows = acc.shape[1], acc.shape[2]

    def bit_of(dim):
        return f if dim == 0 else (r // dim) % 2

    def stride(dim):
        return reps if dim == 0 else dim

    def partner(dim):
        return (1 - f, r) if dim == 0 else (f, across(dim))

    load = pltpu.make_async_copy(weights_hbm, weights, w_sem)
    load.start()
    greet([partner(dim) for dim in [0] + bits])

    spans = [(k * rows, min((k + 1) * rows, size)) for k in range(parts)]
    for p in range(2 * reps):
        for k, (lo, hi) in enumerate(spans):
            if hi < lo + rows:
                acc[p, k] = jnp.zeros((rows, LANES), F32)
            acc[p, k, 0 : hi - lo, :] = flat[p * size + lo : p * size + hi, :]

    def members(fixed, free):
        base = sum(value * stride(dim) for dim, value in fixed)
        out = [base]
        for dim in free:
            out = [i + v * stride(dim) for i in out for v in (0, 1)]
        return out

    pending = {}
    offsets = [0] * parts
    depth = len(bits) + 1
    for stage in range(depth):
        for k in range(parts):
            plan = plans[k]
            dim, free = plan[stage], plan[stage + 1 :]
            settled = [(d, bit_of(d)) for d in plan[:stage]]
            if stage:
                copy, old, count = pending[k]
                copy.wait_recv()
                for j, i in enumerate(members(settled, plan[stage:])):
                    acc[i, k] += rbuf[k, old + j].astype(F32)
            count = 1 << len(free)
            start = offsets[k]
            for j, i in enumerate(members(settled + [(dim, 1 - bit_of(dim))], free)):
                sbuf[k, start + j] = acc[i, k].astype(BF)
            copy = pltpu.make_async_remote_copy(
                src_ref=sbuf.at[k, pl.ds(start, count)], dst_ref=rbuf.at[k, pl.ds(start, count)],
                send_sem=s_send.at[k, stage], recv_sem=s_recv.at[k, stage],
                device_id=partner(dim), device_id_type=MESH,
            )
            copy.start()
            pending.setdefault("all", []).append(copy)
            pending[k] = (copy, start, count)
            offsets[k] = start + count

    me = f * reps + r
    waits = []
    load.wait()
    for k in range(parts):
        copy, old, count = pending[k]
        copy.wait_recv()
        lo, hi = spans[k]
        n = hi - lo
        g = (acc[me, k] + rbuf[k, old].astype(F32))[:n]
        grad[lo:hi, :] = g
        first = beta_one * m_in[lo:hi, :] + (1.0 - beta_one) * g
        second = beta_two * v_in[lo:hi, :] + (1.0 - beta_two) * g * g
        w = weights[pl.ds(r * size + lo, n), :]
        first_hat = first * (1.0 / (1.0 - beta_one**2))
        second_hat = second * (1.0 / (1.0 - beta_two**2))
        change = -learn_rate * (first_hat / (jnp.sqrt(second_hat) + adam_eps) + decay_rate * w)
        if n < rows:
            ag[r, k] = jnp.zeros((rows, LANES), BF)
        ag[r, k, 0:n, :] = change.astype(BF)

    def spread(k, stage):
        plan = [d for d in plans[k] if d > 0][::-1]
        dim = plan[stage]
        fixed = [(d, bit_of(d)) for d in plan[stage:]]
        copies = []
        for j, i in enumerate(members(fixed, plan[:stage])):
            ref = ag.at[i, k]
            at = (1 << stage) - 1 + j
            copies.append(
                pltpu.make_async_remote_copy(
                    src_ref=ref, dst_ref=ref, send_sem=a_send.at[k, at], recv_sem=a_recv.at[k, at],
                    device_id=partner(dim), device_id_type=MESH,
                )
            )
        return copies

    last = {k: [] for k in range(parts)}
    for stage in range(len(bits)):
        for k in range(parts):
            for one in last[k]:
                one.wait_recv()
            last[k] = spread(k, stage)
            for one in last[k]:
                one.start()
            waits += last[k]
    for k in range(parts):
        for one in last[k]:
            one.wait_recv()
    for p in range(reps):
        for k, (lo, hi) in enumerate(spans):
            at = slice(p * size + lo, p * size + hi)
            changes[at, :] = ag[p, k][: hi - lo].astype(F32)
    for one in waits + pending["all"]:
        one.wait_send()


def reduce_update(flat, weights, first_moment, second_moment, reps):
    size = first_moment.shape[0] // LANES
    bits = [1 << i for i in range(reps.bit_length() - 1)]
    parts = len(orders(bits))
    rows = -(-size // (8 * parts)) * 8
    piece = jax.ShapeDtypeStruct((size, LANES), F32)
    stages = len(bits) + 1
    slots = parts * rows * LANES
    held = 4 * reps * size * LANES + slots * (2 * reps * 4 + 4 * 2 * (2 * reps - 1) // 2 + 2 * reps) * 17 // 16
    outs = pl.pallas_call(
        functools.partial(reduce_kernel, reps, size),
        in_specs=[pl.BlockSpec(memory_space=m) for m in (pltpu.VMEM, pl.ANY, pltpu.VMEM, pltpu.VMEM)],
        out_specs=[pl.BlockSpec(memory_space=pltpu.VMEM)] * 2,
        out_shape=[jax.ShapeDtypeStruct((reps * size, LANES), F32), piece],
        scratch_shapes=[
            pltpu.VMEM((reps * size, LANES), F32),
            pltpu.VMEM((2 * reps, parts, rows, LANES), F32),
            pltpu.VMEM((parts, 2 * reps - 1, rows, LANES), BF),
            pltpu.VMEM((parts, 2 * reps - 1, rows, LANES), BF),
            pltpu.VMEM((reps, parts, rows, LANES), BF),
            pltpu.SemaphoreType.DMA,
            pltpu.SemaphoreType.DMA((parts, stages)),
            pltpu.SemaphoreType.DMA((parts, stages)),
            pltpu.SemaphoreType.DMA((parts, reps)),
            pltpu.SemaphoreType.DMA((parts, reps)),
        ],
        compiler_params=pltpu.CompilerParams(
            collective_id=1, has_side_effects=True, vmem_limit_bytes=held + 12 * 2**20
        ),
    )(flat, weights.reshape(-1, LANES), first_moment.reshape(-1, LANES), second_moment.reshape(-1, LANES))
    return [o.reshape(-1) for o in outs]


def on_device(reps, images, cotangent, weights, first_moment, second_moment):
    params = gather_params(weights)
    output, input_grad, flat_grad = compute(images, cotangent, params)
    changes, own_grad = reduce_update(flat_grad, weights, first_moment, second_moment, reps)
    new_weights = weights + changes
    new_first = beta_one * first_moment + (1.0 - beta_one) * own_grad
    new_second = beta_two * second_moment + (1.0 - beta_two) * own_grad * own_grad
    return (output, input_grad, new_weights, own_grad, new_first, new_second)


def solution(mesh):
    in_specs = (
        P(("fsdp", "rep"), None, None),
        P(("fsdp", "rep"), None, None),
        P("fsdp"),
        P(("fsdp", "rep")),
        P(("fsdp", "rep")),
    )
    out_specs = (
        P(("fsdp", "rep"), None, None),
        P(("fsdp", "rep"), None, None),
        P("fsdp"),
        P(("fsdp", "rep")),
        P(("fsdp", "rep")),
        P(("fsdp", "rep")),
    )
    return jax.shard_map(
        functools.partial(on_device, mesh.shape["rep"]), mesh=mesh, in_specs=in_specs, out_specs=out_specs, check_vma=False
    )
```

```python
import functools

import jax
import jax.numpy as jnp
from jax import lax
from jax.experimental import pallas as pl
from jax.experimental.pallas import tpu as pltpu
from jax.sharding import PartitionSpec as P

D = 384
H = 6
FF = 1536
LANES = 128

norm_eps = 1e-06
half_root = 0.7071067811865476
inv_root_two_pi = 0.3989422804014327
beta_one = 0.9
beta_two = 0.999
learn_rate = 0.02
decay_rate = 0.05
adam_eps = 1e-08

AT_QKV = 0
AT_PROJ = AT_QKV + 3 * D * D // LANES
AT_FC1 = AT_PROJ + D * D // LANES
AT_FC2 = AT_FC1 + D * FF // LANES
AT_VEC = AT_FC2 + FF * D // LANES
AT_B1 = AT_VEC + 8 * D // LANES
AT_TAIL = AT_B1 + FF // LANES

BF = jnp.bfloat16
F32 = jnp.float32


def nn(a, b):
    return lax.dot_general(a, b, (((1,), (0,)), ((), ())), preferred_element_type=F32)


def nt(a, b):
    return lax.dot_general(a, b, (((1,), (1,)), ((), ())), preferred_element_type=F32)


def tn(a, b):
    return lax.dot_general(a, b, (((0,), (0,)), ((), ())), preferred_element_type=F32)


def normalize(values):
    centred = values - jnp.mean(values, -1, keepdims=True)
    inverse = lax.rsqrt(jnp.mean(centred * centred, -1, keepdims=True) + norm_eps)
    return centred * inverse, inverse


def normalize_back(d_scaled, scaled, inverse):
    first_mean = jnp.mean(d_scaled, -1, keepdims=True)
    second_mean = jnp.mean(d_scaled * scaled, -1, keepdims=True)
    return (d_scaled - first_mean - scaled * second_mean) * inverse


def columns(x):
    return jnp.sum(x, 0, keepdims=True)


def unpack_into(flat, wq, wp, w1, w2, vec, b1):
    for ref, base in ((wq, AT_QKV), (wp, AT_PROJ), (w1, AT_FC1), (w2, AT_FC2)):
        rows, blocks = ref.shape[0], ref.shape[1] // LANES
        for j in range(blocks):
            ref[:, j * LANES : (j + 1) * LANES] = flat[pl.ds(base + j, rows, stride=blocks), :].astype(BF)
    for c in range(D // LANES):
        vec[:, c * LANES : (c + 1) * LANES] = flat[pl.ds(AT_VEC + c, 8, stride=D // LANES), :]
    for c in range(FF // LANES):
        b1[:, c * LANES : (c + 1) * LANES] = flat[AT_B1 + c : AT_B1 + c + 1, :]


def pack_into(flat, aq, ap, a1, a2, avec, ab1):
    for ref, base in ((aq, AT_QKV), (ap, AT_PROJ), (a1, AT_FC1), (a2, AT_FC2)):
        rows, blocks = ref.shape[0], ref.shape[1] // LANES
        for j in range(blocks):
            flat[pl.ds(base + j, rows, stride=blocks), :] = ref[:, j * LANES : (j + 1) * LANES]
    for c in range(D // LANES):
        flat[pl.ds(AT_VEC + c, 8, stride=D // LANES), :] = avec[:, c * LANES : (c + 1) * LANES]
    for c in range(FF // LANES):
        flat[AT_B1 + c : AT_B1 + c + 1, :] = ab1[:, c * LANES : (c + 1) * LANES]
    flat[AT_TAIL:, :] = jnp.zeros((flat.shape[0] - AT_TAIL, LANES), F32)


def image_step(seq, img, cot, out, dinp, wq, wp, w1, w2, vec, b1, aq, ap, a1, a2, avec, ab1, xs, gs, pf):
    pad = xs.shape[0]
    xs[0:seq, :] = img[0].astype(F32)
    gs[0:seq, :] = cot[0].astype(F32)
    x = xs[...]
    xhat1, inv1 = normalize(x)
    normed1 = (xhat1 * vec[0:1, :] + vec[1:2, :]).astype(BF)
    q = (nn(normed1, wq[:, :D]) + vec[2:3, :]).astype(BF)
    k = nn(normed1, wq[:, D : 2 * D]).astype(BF)
    v = (nn(normed1, wq[:, 2 * D :]) + vec[3:4, :]).astype(BF)
    scale = (D // H) ** (-0.5)
    lane = lax.broadcasted_iota(jnp.int32, (1, LANES), 1)
    halves = [(lane < 64), (lane >= 64)]
    key_ok = lax.broadcasted_iota(jnp.int32, (1, pad), 1) < seq

    def half(block, i):
        return jnp.where(halves[i], block, jnp.zeros_like(block))

    mixed_blocks = []
    for pair in range(D // LANES):
        cut = slice(pair * LANES, (pair + 1) * LANES)
        total = None
        for i in range(2):
            s = nt(half(q[:, cut], i), k[:, cut]) * scale
            s = jnp.where(key_ok, s, -1e30)
            e = jnp.exp(s - jnp.max(s, -1, keepdims=True))
            p = e * (1.0 / jnp.sum(e, -1, keepdims=True))
            pf[2 * pair + i] = p
            term = nn(p.astype(BF), half(v[:, cut], i))
            total = term if total is None else total + term
        mixed_blocks.append(total.astype(BF))
    mixed = jnp.concatenate(mixed_blocks, 1)
    resid = x + nn(mixed, wp[...]) + vec[4:5, :]
    xhat2, inv2 = normalize(resid)
    normed2 = (xhat2 * vec[5:6, :] + vec[6:7, :]).astype(BF)
    dout_f = gs[...]
    dout = dout_f.astype(BF)
    result = resid + vec[7:8, :]
    dnorm2 = None
    step = 512
    for c in range(0, FF, step):
        cut = slice(c, c + step)
        pre = nn(normed2, w1[:, cut]) + b1[:, cut]
        cdf = 0.5 * (1.0 + lax.erf(pre * half_root))
        act = (pre * cdf).astype(BF)
        result = result + nn(act, w2[cut, :])
        a2[cut, :] += tn(act, dout)
        dact = nt(dout, w2[cut, :])
        dpre = dact * (cdf + pre * jnp.exp(-0.5 * pre * pre) * inv_root_two_pi)
        ab1[:, cut] += columns(dpre)
        dpre_b = dpre.astype(BF)
        a1[:, cut] += tn(normed2, dpre_b)
        term = nt(dpre_b, w1[:, cut])
        dnorm2 = term if dnorm2 is None else dnorm2 + term
    out[0] = result.astype(BF)[0:seq, :]
    avec[7:8, :] += columns(dout_f)
    avec[5:6, :] += columns(dnorm2 * xhat2)
    avec[6:7, :] += columns(dnorm2)
    dresid = dout_f + normalize_back(dnorm2 * vec[5:6, :], xhat2, inv2)
    avec[4:5, :] += columns(dresid)
    dresid_b = dresid.astype(BF)
    ap[...] += tn(mixed, dresid_b)
    dmixed = nt(dresid_b, wp[...]).astype(BF)
    dq_blocks, dk_blocks, dv_blocks = [], [], []
    for pair in range(D // LANES):
        cut = slice(pair * LANES, (pair + 1) * LANES)
        dq = dk = dv = None
        for i in range(2):
            p = pf[2 * pair + i]
            dm = half(dmixed[:, cut], i)
            dp = nt(dm, v[:, cut])
            delta = jnp.sum(p * dp, -1, keepdims=True)
            ds = (p * (dp - delta) * scale).astype(BF)
            terms = (
                nn(ds, half(k[:, cut], i)),
                tn(ds, half(q[:, cut], i)),
                tn(p.astype(BF), dm),
            )
            if dq is None:
                dq, dk, dv = terms
            else:
                dq, dk, dv = dq + terms[0], dk + terms[1], dv + terms[2]
        avec[2:3, cut] += columns(dq)
        avec[3:4, cut] += columns(dv)
        dq_blocks.append(dq.astype(BF))
        dk_blocks.append(dk.astype(BF))
        dv_blocks.append(dv.astype(BF))
    dnorm1 = None
    for part, blocks in enumerate((dq_blocks, dk_blocks, dv_blocks)):
        cut = slice(part * D, (part + 1) * D)
        d_part = jnp.concatenate(blocks, 1)
        aq[:, cut] += tn(normed1, d_part)
        term = nt(d_part, wq[:, cut])
        dnorm1 = term if dnorm1 is None else dnorm1 + term
    avec[0:1, :] += columns(dnorm1 * xhat1)
    avec[1:2, :] += columns(dnorm1)
    dx = dresid + normalize_back(dnorm1 * vec[0:1, :], xhat1, inv1)
    dinp[0] = dx.astype(BF)[0:seq, :]


def compute_kernel(seq, img, cot, pflat, out, dinp, gflat, wq, wp, w1, w2, vec, b1, aq, ap, a1, a2, avec, ab1, xs, gs, pf):
    @pl.when(pl.program_id(0) == 0)
    def _():
        gflat[...] = pflat[...].astype(F32)
        unpack_into(gflat, wq, wp, w1, w2, vec, b1)
        for ref in (aq, ap, a1, a2, avec, ab1, xs, gs):
            ref[...] = jnp.zeros_like(ref)

    image_step(seq, img, cot, out, dinp, wq, wp, w1, w2, vec, b1, aq, ap, a1, a2, avec, ab1, xs, gs, pf)

    @pl.when(pl.program_id(0) == pl.num_programs(0) - 1)
    def _():
        pack_into(gflat, aq, ap, a1, a2, avec, ab1)


def compute(images, cotangent, params):
    batch, seq, width = images.shape
    pad = (seq + 15) // 16 * 16
    rows = params.shape[0]
    per_image = pl.BlockSpec((1, seq, width), lambda i: (i, 0, 0))
    whole = pl.BlockSpec(memory_space=pltpu.VMEM)
    mats = [(D, 3 * D), (D, D), (D, FF), (FF, D)]
    vecs = [(8, D), (1, FF)]
    return pl.pallas_call(
        functools.partial(compute_kernel, seq),
        grid=(batch,),
        in_specs=[per_image, per_image, whole],
        out_specs=[per_image, per_image, whole],
        out_shape=[
            jax.ShapeDtypeStruct(images.shape, BF),
            jax.ShapeDtypeStruct(images.shape, BF),
            jax.ShapeDtypeStruct((rows, LANES), F32),
        ],
        scratch_shapes=[pltpu.VMEM(s, BF) for s in mats]
        + [pltpu.VMEM(s, F32) for s in vecs]
        + [pltpu.VMEM(s, F32) for s in mats + vecs]
        + [pltpu.VMEM((pad, width), F32)] * 2
        + [pltpu.VMEM((H, pad, pad), F32)],
        compiler_params=pltpu.CompilerParams(vmem_limit_bytes=36 * 2**20),
    )(images, cotangent, params)


MESH = pl.DeviceIdType.MESH


def place():
    f, r = lax.axis_index("fsdp"), lax.axis_index("rep")

    def across(bit):
        return r + bit * (1 - 2 * ((r // bit) % 2))

    return f, r, across


def greet(partners):
    barrier = pltpu.get_barrier_semaphore()
    for partner in partners:
        pl.semaphore_signal(barrier, inc=1, device_id=partner, device_id_type=MESH)
    pl.semaphore_wait(barrier, len(partners))


def gather_kernel(steps, half, out, wide, wide_sem, send_sem, recv_sem):
    f, r, across = place()
    c, y = r % 2, (r // 2) % 2
    peer, side, core = (1 - f, r), (f, across(2)), (f, across(1))
    mine = (2 * y + c) * steps
    loads = []
    for turn in range(4):
        start = ((2 * y + c + turn) % 4) * steps
        loads.append(
            pltpu.make_async_copy(
                half.at[pl.ds(start, steps)], wide.at[pl.ds(start, steps)], wide_sem.at[turn]
            )
        )
        loads[-1].start()
    greet([peer, side, core])
    sides = (2 * (1 - y) + c) * steps

    def copy(src, dst, kind, s, to):
        return pltpu.make_async_remote_copy(
            src_ref=src, dst_ref=dst, send_sem=send_sem.at[kind, s], recv_sem=recv_sem.at[kind, s],
            device_id=to, device_id_type=MESH,
        )

    first = [copy(out.at[f, mine + s], out.at[f, mine + s], 0, s, peer) for s in range(steps)]
    loads[0].wait()
    for s in range(steps):
        out[f, mine + s] = wide[mine + s].astype(BF)
        first[s].start()
    for turn in range(1, 4):
        loads[turn].wait()
        start = ((2 * y + c + turn) % 4) * steps
        for s in range(steps):
            out[f, start + s] = wide[start + s].astype(BF)

    def relay(kind, s, base, to):
        ref = out.at[1 - f, base + s]
        return copy(ref, ref, kind, s, to)

    second = [relay(1, s, mine, side) for s in range(steps)]
    third = [relay(2, s, mine, core) for s in range(steps)]
    fourth = [relay(3, s, sides, core) for s in range(steps)]
    for s in range(steps):
        first[s].wait_recv()
        second[s].start()
        third[s].start()
    for s in range(steps):
        second[s].wait_recv()
        fourth[s].start()
    for s in range(steps):
        third[s].wait_recv()
        fourth[s].wait_recv()
    for group in (first, second, third, fourth):
        for one in group:
            one.wait_send()


def gather_params(half):
    rows = half.shape[0] // LANES
    quarter = rows // 4
    steps = next(s for s in (7, 5, 4, 3, 2, 1) if quarter % (8 * s) == 0)
    shape = (4 * steps, quarter // steps, LANES)
    out = pl.pallas_call(
        functools.partial(gather_kernel, steps),
        in_specs=[pl.BlockSpec(memory_space=pltpu.HBM)],
        out_specs=pl.BlockSpec(memory_space=pltpu.VMEM),
        out_shape=jax.ShapeDtypeStruct((2,) + shape, BF),
        scratch_shapes=[
            pltpu.VMEM(shape, F32),
            pltpu.SemaphoreType.DMA((4,)),
            pltpu.SemaphoreType.DMA((4, steps)),
            pltpu.SemaphoreType.DMA((4, steps)),
        ],
        compiler_params=pltpu.CompilerParams(collective_id=0, has_side_effects=True, vmem_limit_bytes=16 * 2**20),
    )(half.reshape(shape))
    return out.reshape(2 * rows, LANES)


def orders(bits):
    rest = [b for b in bits if b > 1]
    low, high = rest[:2], rest[2:]
    dims = [0] + low
    return [[1] + dims[i:] + dims[:i] + high for i in range(len(dims))]


def reduce_kernel(
    reps, size, flat, weights_hbm, m_in, v_in, changes, grad, weights, acc, sbuf, rbuf, ag, w_sem, s_send, s_recv, a_send, a_recv
):
    f, r, across = place()
    bits = [1 << i for i in range(reps.bit_length() - 1)]
    plans = orders(bits)
    parts, rows = acc.shape[1], acc.shape[2]

    def bit_of(dim):
        return f if dim == 0 else (r // dim) % 2

    def stride(dim):
        return reps if dim == 0 else dim

    def partner(dim):
        return (1 - f, r) if dim == 0 else (f, across(dim))

    load = pltpu.make_async_copy(weights_hbm, weights, w_sem)
    load.start()
    greet([partner(dim) for dim in [0] + bits])

    spans = [(k * rows, min((k + 1) * rows, size)) for k in range(parts)]

    def pack(k):
        lo, hi = spans[k]
        for p in range(2 * reps):
            if hi < lo + rows:
                acc[p, k, (hi - lo) // 8 * 8 :, :] = jnp.zeros((rows - (hi - lo) // 8 * 8, LANES), F32)
            acc[p, k, 0 : hi - lo, :] = flat[p * size + lo : p * size + hi, :]

    def members(fixed, free):
        base = sum(value * stride(dim) for dim, value in fixed)
        out = [base]
        for dim in free:
            out = [i + v * stride(dim) for i in out for v in (0, 1)]
        return out

    pending = {}
    offsets = [0] * parts
    depth = len(bits) + 1
    for stage in range(depth):
        for k in range(parts):
            plan = plans[k]
            dim, free = plan[stage], plan[stage + 1 :]
            settled = [(d, bit_of(d)) for d in plan[:stage]]
            if stage == 0:
                pack(k)
            else:
                copy, old, count = pending[k]
                copy.wait_recv()
                for j, i in enumerate(members(settled, plan[stage:])):
                    acc[i, k] += rbuf[k, old + j].astype(F32)
            count = 1 << len(free)
            start = offsets[k]
            for j, i in enumerate(members(settled + [(dim, 1 - bit_of(dim))], free)):
                sbuf[k, start + j] = acc[i, k].astype(BF)
            copy = pltpu.make_async_remote_copy(
                src_ref=sbuf.at[k, pl.ds(start, count)], dst_ref=rbuf.at[k, pl.ds(start, count)],
                send_sem=s_send.at[k, stage], recv_sem=s_recv.at[k, stage],
                device_id=partner(dim), device_id_type=MESH,
            )
            copy.start()
            pending.setdefault("all", []).append(copy)
            pending[k] = (copy, start, count)
            offsets[k] = start + count

    me = f * reps + r
    def spread(k, stage):
        plan = [d for d in plans[k] if d > 0][::-1]
        dim = plan[stage]
        fixed = [(d, bit_of(d)) for d in plan[stage:]]
        copies = []
        for j, i in enumerate(members(fixed, plan[:stage])):
            ref = ag.at[i, k]
            at = (1 << stage) - 1 + j
            copies.append(
                pltpu.make_async_remote_copy(
                    src_ref=ref, dst_ref=ref, send_sem=a_send.at[k, at], recv_sem=a_recv.at[k, at],
                    device_id=partner(dim), device_id_type=MESH,
                )
            )
        return copies

    last = {}
    waits = []
    load.wait()
    for k in range(parts):
        copy, old, count = pending[k]
        copy.wait_recv()
        lo, hi = spans[k]
        n = hi - lo
        g = (acc[me, k] + rbuf[k, old].astype(F32))[:n]
        grad[lo:hi, :] = g
        first = beta_one * m_in[lo:hi, :] + (1.0 - beta_one) * g
        second = beta_two * v_in[lo:hi, :] + (1.0 - beta_two) * g * g
        w = weights[pl.ds(r * size + lo, n), :]
        first_hat = first * (1.0 / (1.0 - beta_one**2))
        second_hat = second * (1.0 / (1.0 - beta_two**2))
        change = -learn_rate * (first_hat / (jnp.sqrt(second_hat) + adam_eps) + decay_rate * w)
        if n < rows:
            ag[r, k] = jnp.zeros((rows, LANES), BF)
        ag[r, k, 0:n, :] = change.astype(BF)
        last[k] = spread(k, 0)
        for one in last[k]:
            one.start()
        waits += last[k]

    for stage in range(1, len(bits)):
        for k in range(parts):
            for one in last[k]:
                one.wait_recv()
            last[k] = spread(k, stage)
            for one in last[k]:
                one.start()
            waits += last[k]
    for k, (lo, hi) in enumerate(spans):
        for one in last[k]:
            one.wait_recv()
        for p in range(reps):
            at = slice(p * size + lo, p * size + hi)
            changes[at, :] = ag[p, k][: hi - lo].astype(F32)
    for one in waits + pending["all"]:
        one.wait_send()


def reduce_update(flat, weights, first_moment, second_moment, reps):
    size = first_moment.shape[0] // LANES
    bits = [1 << i for i in range(reps.bit_length() - 1)]
    parts = len(orders(bits))
    rows = -(-size // (8 * parts)) * 8
    piece = jax.ShapeDtypeStruct((size, LANES), F32)
    stages = len(bits) + 1
    slots = parts * rows * LANES
    held = 4 * reps * size * LANES + slots * (2 * reps * 4 + 4 * 2 * (2 * reps - 1) // 2 + 2 * reps) * 17 // 16
    outs = pl.pallas_call(
        functools.partial(reduce_kernel, reps, size),
        in_specs=[pl.BlockSpec(memory_space=m) for m in (pltpu.VMEM, pl.ANY, pltpu.VMEM, pltpu.VMEM)],
        out_specs=[pl.BlockSpec(memory_space=pltpu.VMEM)] * 2,
        out_shape=[jax.ShapeDtypeStruct((reps * size, LANES), F32), piece],
        scratch_shapes=[
            pltpu.VMEM((reps * size, LANES), F32),
            pltpu.VMEM((2 * reps, parts, rows, LANES), F32),
            pltpu.VMEM((parts, 2 * reps - 1, rows, LANES), BF),
            pltpu.VMEM((parts, 2 * reps - 1, rows, LANES), BF),
            pltpu.VMEM((reps, parts, rows, LANES), BF),
            pltpu.SemaphoreType.DMA,
            pltpu.SemaphoreType.DMA((parts, stages)),
            pltpu.SemaphoreType.DMA((parts, stages)),
            pltpu.SemaphoreType.DMA((parts, reps)),
            pltpu.SemaphoreType.DMA((parts, reps)),
        ],
        compiler_params=pltpu.CompilerParams(
            collective_id=1, has_side_effects=True, vmem_limit_bytes=held + 12 * 2**20
        ),
    )(flat, weights.reshape(-1, LANES), first_moment.reshape(-1, LANES), second_moment.reshape(-1, LANES))
    return [o.reshape(-1) for o in outs]


def on_device(reps, images, cotangent, weights, first_moment, second_moment):
    params = gather_params(weights)
    output, input_grad, flat_grad = compute(images, cotangent, params)
    changes, own_grad = reduce_update(flat_grad, weights, first_moment, second_moment, reps)
    new_weights = weights + changes
    new_first = beta_one * first_moment + (1.0 - beta_one) * own_grad
    new_second = beta_two * second_moment + (1.0 - beta_two) * own_grad * own_grad
    return (output, input_grad, new_weights, own_grad, new_first, new_second)


def solution(mesh):
    in_specs = (
        P(("fsdp", "rep"), None, None),
        P(("fsdp", "rep"), None, None),
        P("fsdp"),
        P(("fsdp", "rep")),
        P(("fsdp", "rep")),
    )
    out_specs = (
        P(("fsdp", "rep"), None, None),
        P(("fsdp", "rep"), None, None),
        P("fsdp"),
        P(("fsdp", "rep")),
        P(("fsdp", "rep")),
        P(("fsdp", "rep")),
    )
    return jax.shard_map(
        functools.partial(on_device, mesh.shape["rep"]), mesh=mesh, in_specs=in_specs, out_specs=out_specs, check_vma=False
    )
```

```python
import functools

import jax
import jax.numpy as jnp
from jax import lax
from jax.experimental import pallas as pl
from jax.experimental.pallas import tpu as pltpu
from jax.sharding import PartitionSpec as P

D = 384
H = 6
FF = 1536
LANES = 128

norm_eps = 1e-06
half_root = 0.7071067811865476
inv_root_two_pi = 0.3989422804014327
beta_one = 0.9
beta_two = 0.999
learn_rate = 0.02
decay_rate = 0.05
adam_eps = 1e-08

AT_QKV = 0
AT_PROJ = AT_QKV + 3 * D * D // LANES
AT_FC1 = AT_PROJ + D * D // LANES
AT_FC2 = AT_FC1 + D * FF // LANES
AT_VEC = AT_FC2 + FF * D // LANES
AT_B1 = AT_VEC + 8 * D // LANES
AT_TAIL = AT_B1 + FF // LANES

BF = jnp.bfloat16
F32 = jnp.float32


def nn(a, b):
    return lax.dot_general(a, b, (((1,), (0,)), ((), ())), preferred_element_type=F32)


def nt(a, b):
    return lax.dot_general(a, b, (((1,), (1,)), ((), ())), preferred_element_type=F32)


def tn(a, b):
    return lax.dot_general(a, b, (((0,), (0,)), ((), ())), preferred_element_type=F32)


def normalize(values):
    centred = values - jnp.mean(values, -1, keepdims=True)
    inverse = lax.rsqrt(jnp.mean(centred * centred, -1, keepdims=True) + norm_eps)
    return centred * inverse, inverse


def normalize_back(d_scaled, scaled, inverse):
    first_mean = jnp.mean(d_scaled, -1, keepdims=True)
    second_mean = jnp.mean(d_scaled * scaled, -1, keepdims=True)
    return (d_scaled - first_mean - scaled * second_mean) * inverse


def columns(x):
    return jnp.sum(x, 0, keepdims=True)


def unpack_into(flat, wq, wp, w1, w2, vec, b1):
    for ref, base in ((wq, AT_QKV), (wp, AT_PROJ), (w1, AT_FC1), (w2, AT_FC2)):
        rows, blocks = ref.shape[0], ref.shape[1] // LANES
        for j in range(blocks):
            ref[:, j * LANES : (j + 1) * LANES] = flat[pl.ds(base + j, rows, stride=blocks), :].astype(BF)
    for c in range(D // LANES):
        vec[:, c * LANES : (c + 1) * LANES] = flat[pl.ds(AT_VEC + c, 8, stride=D // LANES), :]
    for c in range(FF // LANES):
        b1[:, c * LANES : (c + 1) * LANES] = flat[AT_B1 + c : AT_B1 + c + 1, :]


def pack_into(flat, aq, ap, a1, a2, avec, ab1):
    for ref, base in ((aq, AT_QKV), (ap, AT_PROJ), (a1, AT_FC1), (a2, AT_FC2)):
        rows, blocks = ref.shape[0], ref.shape[1] // LANES
        for j in range(blocks):
            flat[pl.ds(base + j, rows, stride=blocks), :] = ref[:, j * LANES : (j + 1) * LANES]
    for c in range(D // LANES):
        flat[pl.ds(AT_VEC + c, 8, stride=D // LANES), :] = avec[:, c * LANES : (c + 1) * LANES]
    for c in range(FF // LANES):
        flat[AT_B1 + c : AT_B1 + c + 1, :] = ab1[:, c * LANES : (c + 1) * LANES]
    flat[AT_TAIL:, :] = jnp.zeros((flat.shape[0] - AT_TAIL, LANES), F32)


def image_step(seq, img, cot, out, dinp, wq, wp, w1, w2, vec, b1, aq, ap, a1, a2, avec, ab1, xs, gs, pf):
    pad = xs.shape[0]
    xs[0:seq, :] = img[0].astype(F32)
    gs[0:seq, :] = cot[0].astype(F32)
    x = xs[...]
    xhat1, inv1 = normalize(x)
    normed1 = (xhat1 * vec[0:1, :] + vec[1:2, :]).astype(BF)
    q = (nn(normed1, wq[:, :D]) + vec[2:3, :]).astype(BF)
    k = nn(normed1, wq[:, D : 2 * D]).astype(BF)
    v = (nn(normed1, wq[:, 2 * D :]) + vec[3:4, :]).astype(BF)
    scale = (D // H) ** (-0.5)
    lane = lax.broadcasted_iota(jnp.int32, (1, LANES), 1)
    halves = [(lane < 64), (lane >= 64)]
    key_ok = lax.broadcasted_iota(jnp.int32, (1, pad), 1) < seq

    def half(block, i):
        return jnp.where(halves[i], block, jnp.zeros_like(block))

    mixed_blocks = []
    for pair in range(D // LANES):
        cut = slice(pair * LANES, (pair + 1) * LANES)
        total = None
        for i in range(2):
            s = nt(half(q[:, cut], i), k[:, cut]) * scale
            s = jnp.where(key_ok, s, -1e30)
            e = jnp.exp(s - jnp.max(s, -1, keepdims=True))
            p = e * (1.0 / jnp.sum(e, -1, keepdims=True))
            pf[2 * pair + i] = p
            term = nn(p.astype(BF), half(v[:, cut], i))
            total = term if total is None else total + term
        mixed_blocks.append(total.astype(BF))
    mixed = jnp.concatenate(mixed_blocks, 1)
    resid = x + nn(mixed, wp[...]) + vec[4:5, :]
    xhat2, inv2 = normalize(resid)
    normed2 = (xhat2 * vec[5:6, :] + vec[6:7, :]).astype(BF)
    dout_f = gs[...]
    dout = dout_f.astype(BF)
    result = resid + vec[7:8, :]
    dnorm2 = None
    step = 768
    for c in range(0, FF, step):
        cut = slice(c, c + step)
        pre = nn(normed2, w1[:, cut]) + b1[:, cut]
        cdf = 0.5 * (1.0 + lax.erf(pre * half_root))
        act = (pre * cdf).astype(BF)
        result = result + nn(act, w2[cut, :])
        a2[cut, :] += tn(act, dout)
        dact = nt(dout, w2[cut, :])
        dpre = dact * (cdf + pre * jnp.exp(-0.5 * pre * pre) * inv_root_two_pi)
        ab1[:, cut] += columns(dpre)
        dpre_b = dpre.astype(BF)
        a1[:, cut] += tn(normed2, dpre_b)
        term = nt(dpre_b, w1[:, cut])
        dnorm2 = term if dnorm2 is None else dnorm2 + term
    out[0] = result.astype(BF)[0:seq, :]
    avec[7:8, :] += columns(dout_f)
    avec[5:6, :] += columns(dnorm2 * xhat2)
    avec[6:7, :] += columns(dnorm2)
    dresid = dout_f + normalize_back(dnorm2 * vec[5:6, :], xhat2, inv2)
    avec[4:5, :] += columns(dresid)
    dresid_b = dresid.astype(BF)
    ap[...] += tn(mixed, dresid_b)
    dmixed = nt(dresid_b, wp[...]).astype(BF)
    dq_blocks, dk_blocks, dv_blocks = [], [], []
    for pair in range(D // LANES):
        cut = slice(pair * LANES, (pair + 1) * LANES)
        dq = dk = dv = None
        for i in range(2):
            p = pf[2 * pair + i]
            dm = half(dmixed[:, cut], i)
            dp = nt(dm, v[:, cut])
            delta = jnp.sum(p * dp, -1, keepdims=True)
            ds = (p * (dp - delta) * scale).astype(BF)
            terms = (
                nn(ds, half(k[:, cut], i)),
                tn(ds, half(q[:, cut], i)),
                tn(p.astype(BF), dm),
            )
            if dq is None:
                dq, dk, dv = terms
            else:
                dq, dk, dv = dq + terms[0], dk + terms[1], dv + terms[2]
        avec[2:3, cut] += columns(dq)
        avec[3:4, cut] += columns(dv)
        dq_blocks.append(dq.astype(BF))
        dk_blocks.append(dk.astype(BF))
        dv_blocks.append(dv.astype(BF))
    dnorm1 = None
    for part, blocks in enumerate((dq_blocks, dk_blocks, dv_blocks)):
        cut = slice(part * D, (part + 1) * D)
        d_part = jnp.concatenate(blocks, 1)
        aq[:, cut] += tn(normed1, d_part)
        term = nt(d_part, wq[:, cut])
        dnorm1 = term if dnorm1 is None else dnorm1 + term
    avec[0:1, :] += columns(dnorm1 * xhat1)
    avec[1:2, :] += columns(dnorm1)
    dx = dresid + normalize_back(dnorm1 * vec[0:1, :], xhat1, inv1)
    dinp[0] = dx.astype(BF)[0:seq, :]


def compute_kernel(seq, img, cot, pflat, out, dinp, gflat, wq, wp, w1, w2, vec, b1, aq, ap, a1, a2, avec, ab1, xs, gs, pf):
    @pl.when(pl.program_id(0) == 0)
    def _():
        gflat[...] = pflat[...].astype(F32)
        unpack_into(gflat, wq, wp, w1, w2, vec, b1)
        for ref in (aq, ap, a1, a2, avec, ab1, xs, gs):
            ref[...] = jnp.zeros_like(ref)

    image_step(seq, img, cot, out, dinp, wq, wp, w1, w2, vec, b1, aq, ap, a1, a2, avec, ab1, xs, gs, pf)

    @pl.when(pl.program_id(0) == pl.num_programs(0) - 1)
    def _():
        pack_into(gflat, aq, ap, a1, a2, avec, ab1)


def compute(images, cotangent, params):
    batch, seq, width = images.shape
    pad = (seq + 15) // 16 * 16
    rows = params.shape[0]
    per_image = pl.BlockSpec((1, seq, width), lambda i: (i, 0, 0))
    whole = pl.BlockSpec(memory_space=pltpu.VMEM)
    mats = [(D, 3 * D), (D, D), (D, FF), (FF, D)]
    vecs = [(8, D), (1, FF)]
    return pl.pallas_call(
        functools.partial(compute_kernel, seq),
        grid=(batch,),
        in_specs=[per_image, per_image, whole],
        out_specs=[per_image, per_image, whole],
        out_shape=[
            jax.ShapeDtypeStruct(images.shape, BF),
            jax.ShapeDtypeStruct(images.shape, BF),
            jax.ShapeDtypeStruct((rows, LANES), F32),
        ],
        scratch_shapes=[pltpu.VMEM(s, BF) for s in mats]
        + [pltpu.VMEM(s, F32) for s in vecs]
        + [pltpu.VMEM(s, F32) for s in mats + vecs]
        + [pltpu.VMEM((pad, width), F32)] * 2
        + [pltpu.VMEM((H, pad, pad), F32)],
        compiler_params=pltpu.CompilerParams(vmem_limit_bytes=36 * 2**20),
    )(images, cotangent, params)


MESH = pl.DeviceIdType.MESH


def place():
    f, r = lax.axis_index("fsdp"), lax.axis_index("rep")

    def across(bit):
        return r + bit * (1 - 2 * ((r // bit) % 2))

    return f, r, across


def greet(partners):
    barrier = pltpu.get_barrier_semaphore()
    for partner in partners:
        pl.semaphore_signal(barrier, inc=1, device_id=partner, device_id_type=MESH)
    pl.semaphore_wait(barrier, len(partners))


def gather_kernel(steps, half, out, wide, wide_sem, send_sem, recv_sem):
    f, r, across = place()
    c, y = r % 2, (r // 2) % 2
    peer, side, core = (1 - f, r), (f, across(2)), (f, across(1))
    mine = (2 * y + c) * steps
    loads = []
    for turn in range(4):
        start = ((2 * y + c + turn) % 4) * steps
        loads.append(
            pltpu.make_async_copy(
                half.at[pl.ds(start, steps)], wide.at[pl.ds(start, steps)], wide_sem.at[turn]
            )
        )
        loads[-1].start()
    greet([peer, side, core])
    sides = (2 * (1 - y) + c) * steps

    def copy(src, dst, kind, s, to):
        return pltpu.make_async_remote_copy(
            src_ref=src, dst_ref=dst, send_sem=send_sem.at[kind, s], recv_sem=recv_sem.at[kind, s],
            device_id=to, device_id_type=MESH,
        )

    first = [copy(out.at[f, mine + s], out.at[f, mine + s], 0, s, peer) for s in range(steps)]
    loads[0].wait()
    for s in range(steps):
        out[f, mine + s] = wide[mine + s].astype(BF)
        first[s].start()
    for turn in range(1, 4):
        loads[turn].wait()
        start = ((2 * y + c + turn) % 4) * steps
        for s in range(steps):
            out[f, start + s] = wide[start + s].astype(BF)

    def relay(kind, s, base, to):
        ref = out.at[1 - f, base + s]
        return copy(ref, ref, kind, s, to)

    second = [relay(1, s, mine, side) for s in range(steps)]
    third = [relay(2, s, mine, core) for s in range(steps)]
    fourth = [relay(3, s, sides, core) for s in range(steps)]
    for s in range(steps):
        first[s].wait_recv()
        second[s].start()
        third[s].start()
    for s in range(steps):
        second[s].wait_recv()
        fourth[s].start()
    for s in range(steps):
        third[s].wait_recv()
        fourth[s].wait_recv()
    for group in (first, second, third, fourth):
        for one in group:
            one.wait_send()


def gather_params(half):
    rows = half.shape[0] // LANES
    quarter = rows // 4
    steps = next(s for s in (7, 5, 4, 3, 2, 1) if quarter % (8 * s) == 0)
    shape = (4 * steps, quarter // steps, LANES)
    out = pl.pallas_call(
        functools.partial(gather_kernel, steps),
        in_specs=[pl.BlockSpec(memory_space=pltpu.HBM)],
        out_specs=pl.BlockSpec(memory_space=pltpu.VMEM),
        out_shape=jax.ShapeDtypeStruct((2,) + shape, BF),
        scratch_shapes=[
            pltpu.VMEM(shape, F32),
            pltpu.SemaphoreType.DMA((4,)),
            pltpu.SemaphoreType.DMA((4, steps)),
            pltpu.SemaphoreType.DMA((4, steps)),
        ],
        compiler_params=pltpu.CompilerParams(collective_id=0, has_side_effects=True, vmem_limit_bytes=16 * 2**20),
    )(half.reshape(shape))
    return out.reshape(2 * rows, LANES)


def orders(bits):
    rest = [b for b in bits if b > 1]
    low, high = rest[:2], rest[2:]
    dims = [0] + low
    return [[1] + dims[i:] + dims[:i] + high for i in range(len(dims))]


def reduce_kernel(
    reps, size, flat, weights_hbm, m_in, v_in, changes, grad, weights, acc, sbuf, rbuf, ag, w_sem, s_send, s_recv, a_send, a_recv
):
    f, r, across = place()
    bits = [1 << i for i in range(reps.bit_length() - 1)]
    plans = orders(bits)
    parts, rows = acc.shape[1], acc.shape[2]

    def bit_of(dim):
        return f if dim == 0 else (r // dim) % 2

    def stride(dim):
        return reps if dim == 0 else dim

    def partner(dim):
        return (1 - f, r) if dim == 0 else (f, across(dim))

    load = pltpu.make_async_copy(weights_hbm, weights, w_sem)
    load.start()
    greet([partner(dim) for dim in [0] + bits])

    spans = [(k * rows, min((k + 1) * rows, size)) for k in range(parts)]

    def pack(k):
        lo, hi = spans[k]
        for p in range(2 * reps):
            if hi < lo + rows:
                acc[p, k, (hi - lo) // 8 * 8 :, :] = jnp.zeros((rows - (hi - lo) // 8 * 8, LANES), F32)
            acc[p, k, 0 : hi - lo, :] = flat[p * size + lo : p * size + hi, :]

    def members(fixed, free):
        base = sum(value * stride(dim) for dim, value in fixed)
        out = [base]
        for dim in free:
            out = [i + v * stride(dim) for i in out for v in (0, 1)]
        return out

    pending = {}
    offsets = [0] * parts
    depth = len(bits) + 1
    for stage in range(depth):
        for k in range(parts):
            plan = plans[k]
            dim, free = plan[stage], plan[stage + 1 :]
            settled = [(d, bit_of(d)) for d in plan[:stage]]
            if stage == 0:
                pack(k)
            else:
                copy, old, count = pending[k]
                copy.wait_recv()
                for j, i in enumerate(members(settled, plan[stage:])):
                    acc[i, k] += rbuf[k, old + j].astype(F32)
            count = 1 << len(free)
            start = offsets[k]
            for j, i in enumerate(members(settled + [(dim, 1 - bit_of(dim))], free)):
                sbuf[k, start + j] = acc[i, k].astype(BF)
            copy = pltpu.make_async_remote_copy(
                src_ref=sbuf.at[k, pl.ds(start, count)], dst_ref=rbuf.at[k, pl.ds(start, count)],
                send_sem=s_send.at[k, stage], recv_sem=s_recv.at[k, stage],
                device_id=partner(dim), device_id_type=MESH,
            )
            copy.start()
            pending.setdefault("all", []).append(copy)
            pending[k] = (copy, start, count)
            offsets[k] = start + count

    me = f * reps + r
    def spread(k, stage):
        plan = [d for d in plans[k] if d > 0][::-1]
        dim = plan[stage]
        fixed = [(d, bit_of(d)) for d in plan[stage:]]
        copies = []
        for j, i in enumerate(members(fixed, plan[:stage])):
            ref = ag.at[i, k]
            at = (1 << stage) - 1 + j
            copies.append(
                pltpu.make_async_remote_copy(
                    src_ref=ref, dst_ref=ref, send_sem=a_send.at[k, at], recv_sem=a_recv.at[k, at],
                    device_id=partner(dim), device_id_type=MESH,
                )
            )
        return copies

    last = {}
    waits = []
    load.wait()
    for k in range(parts):
        copy, old, count = pending[k]
        copy.wait_recv()
        lo, hi = spans[k]
        n = hi - lo
        g = (acc[me, k] + rbuf[k, old].astype(F32))[:n]
        grad[lo:hi, :] = g
        first = beta_one * m_in[lo:hi, :] + (1.0 - beta_one) * g
        second = beta_two * v_in[lo:hi, :] + (1.0 - beta_two) * g * g
        w = weights[pl.ds(r * size + lo, n), :]
        first_hat = first * (1.0 / (1.0 - beta_one**2))
        second_hat = second * (1.0 / (1.0 - beta_two**2))
        change = -learn_rate * (first_hat / (jnp.sqrt(second_hat) + adam_eps) + decay_rate * w)
        if n < rows:
            ag[r, k] = jnp.zeros((rows, LANES), BF)
        ag[r, k, 0:n, :] = change.astype(BF)
        last[k] = spread(k, 0)
        for one in last[k]:
            one.start()
        waits += last[k]

    for stage in range(1, len(bits)):
        for k in range(parts):
            for one in last[k]:
                one.wait_recv()
            last[k] = spread(k, stage)
            for one in last[k]:
                one.start()
            waits += last[k]
    for k, (lo, hi) in enumerate(spans):
        for one in last[k]:
            one.wait_recv()
        for p in range(reps):
            at = slice(p * size + lo, p * size + hi)
            changes[at, :] = ag[p, k][: hi - lo].astype(F32)
    for one in waits + pending["all"]:
        one.wait_send()


def reduce_update(flat, weights, first_moment, second_moment, reps):
    size = first_moment.shape[0] // LANES
    bits = [1 << i for i in range(reps.bit_length() - 1)]
    parts = len(orders(bits))
    rows = -(-size // (8 * parts)) * 8
    piece = jax.ShapeDtypeStruct((size, LANES), F32)
    stages = len(bits) + 1
    slots = parts * rows * LANES
    held = 4 * reps * size * LANES + slots * (2 * reps * 4 + 4 * 2 * (2 * reps - 1) // 2 + 2 * reps) * 17 // 16
    outs = pl.pallas_call(
        functools.partial(reduce_kernel, reps, size),
        in_specs=[pl.BlockSpec(memory_space=m) for m in (pltpu.VMEM, pl.ANY, pltpu.VMEM, pltpu.VMEM)],
        out_specs=[pl.BlockSpec(memory_space=pltpu.VMEM)] * 2,
        out_shape=[jax.ShapeDtypeStruct((reps * size, LANES), F32), piece],
        scratch_shapes=[
            pltpu.VMEM((reps * size, LANES), F32),
            pltpu.VMEM((2 * reps, parts, rows, LANES), F32),
            pltpu.VMEM((parts, 2 * reps - 1, rows, LANES), BF),
            pltpu.VMEM((parts, 2 * reps - 1, rows, LANES), BF),
            pltpu.VMEM((reps, parts, rows, LANES), BF),
            pltpu.SemaphoreType.DMA,
            pltpu.SemaphoreType.DMA((parts, stages)),
            pltpu.SemaphoreType.DMA((parts, stages)),
            pltpu.SemaphoreType.DMA((parts, reps)),
            pltpu.SemaphoreType.DMA((parts, reps)),
        ],
        compiler_params=pltpu.CompilerParams(
            collective_id=1, has_side_effects=True, vmem_limit_bytes=held + 12 * 2**20
        ),
    )(flat, weights.reshape(-1, LANES), first_moment.reshape(-1, LANES), second_moment.reshape(-1, LANES))
    return [o.reshape(-1) for o in outs]


def on_device(reps, images, cotangent, weights, first_moment, second_moment):
    params = gather_params(weights)
    output, input_grad, flat_grad = compute(images, cotangent, params)
    changes, own_grad = reduce_update(flat_grad, weights, first_moment, second_moment, reps)
    new_weights = weights + changes
    new_first = beta_one * first_moment + (1.0 - beta_one) * own_grad
    new_second = beta_two * second_moment + (1.0 - beta_two) * own_grad * own_grad
    return (output, input_grad, new_weights, own_grad, new_first, new_second)


def solution(mesh):
    in_specs = (
        P(("fsdp", "rep"), None, None),
        P(("fsdp", "rep"), None, None),
        P("fsdp"),
        P(("fsdp", "rep")),
        P(("fsdp", "rep")),
    )
    out_specs = (
        P(("fsdp", "rep"), None, None),
        P(("fsdp", "rep"), None, None),
        P("fsdp"),
        P(("fsdp", "rep")),
        P(("fsdp", "rep")),
        P(("fsdp", "rep")),
    )
    return jax.shard_map(
        functools.partial(on_device, mesh.shape["rep"]), mesh=mesh, in_specs=in_specs, out_specs=out_specs, check_vma=False
    )
```
